256 devices in a mesh: rep: 2 (over core), req: 32 (over y, z), tp: 4 (over x).
Axes of the slice: x: 4, y: 4, z: 8, core: 2. Of those that a mesh axis runs over, the one named last changes fastest.
Arguments:
- hidden: bfloat16 [1024, 1536], P(('rep', 'req'), 'tp'), may hold values from -6 to 6
- lengths: int32 [2, 512], P(None, 'req'), may hold values from 16 to 1024, as said below
- migrate: int32 [32], P('req'), may hold values from 0 to 15
- kv_cache: bfloat16 [1024, 1024, 8, 128], P(('rep', 'req'), None, 'tp'), may hold values from -250 to 250
- attn_gain: float32 [1536], replicated, may hold values from 0.1 to 1.9
- moe_gain: float32 [1536], replicated, may hold values from 0.1 to 1.9
- w_query: bfloat16 [1536, 1536], P(None, 'tp'), may hold values from -0.15625 to 0.15625
- key_value_weight: bfloat16 [1536, 1024], P(None, 'tp'), may hold values from -0.15625 to 0.15625
- output_weight: bfloat16 [1536, 1536], P('tp'), may hold values from -0.25 to 0.25
- w_gateup: bfloat16 [64, 1536, 2, 512], P(('rep', 'req'), None, None, 'tp'), may hold values from -0.15625 to 0.15625
- w_down: bfloat16 [64, 512, 1536], P(('rep', 'req'), 'tp'), may hold values from -0.25 to 0.25
- expert_ids: int32 [1024, 8], P(('rep', 'req')), may hold values from 0 to 63, all different within a row; in each aligned block of 16 rows (0 to 15, 16 to 31, ...) at most 6 rows name the same one
- expert_gates: float32 [1024, 8], P(('rep', 'req')), may hold values from 0.1 to 0.4
Outputs:
- layer_out: bfloat16 [1024, 1536], P(('rep', 'req'), 'tp')
The draws below stay inside these ranges and needn't reach their ends.
Inputs may be any that keep to these rules, and one draw needn't show every extreme that they name: A request attends to its first lengths positions and to its own new key. `expert_ids`: each row names 8 distinct experts; among the rows of one device (an aligned block of 16 rows) no expert is named more than 6 times, and in some blocks one expert is named exactly 6 times.
All inputs are finite; a program needn't handle non-finite values.
Results may differ from the reference program's by a relative error of at most 0.015.
Values may be sent and summed in bfloat16 or wider, within the bound.
A program may use at most 64 MiB of HBM per device.

```python
import math
import jax
import jax.numpy as jnp
import numpy as np
from jax import lax

MODEL_DIM = 1536
QUERY_HEADS = 24
KEY_VALUE_HEADS = 8
HEAD_SIZE = 64
EXP_HID = 512
TOPK = 8
RQ_DEV = 16
CONTEXT_SLOTS = 1024
REQUEST_TOTAL = 1024
EXPERTS = 64
CAP = 6
N_REP = 2
N_REQ = 32


def draw_lengths(key, part):
    top_bits = CONTEXT_SLOTS.bit_length() - 1
    first_key, second_key = jax.random.split(key)
    complete_shape = (N_REP, REQUEST_TOTAL // N_REP)
    exponent = jax.random.randint(first_key, complete_shape, 4, top_bits + 1)
    floor_len = jnp.left_shift(jnp.ones(complete_shape, jnp.int32), exponent)
    offset = jax.random.randint(second_key, complete_shape, 0, 1 << 30) % floor_len
    drawn = jnp.minimum(floor_len + offset, CONTEXT_SLOTS)
    return drawn.at[0, 0].set(CONTEXT_SLOTS)


def draw_kv_cache(key, part):
    complete_shape = (REQUEST_TOTAL, CONTEXT_SLOTS, KEY_VALUE_HEADS, 2 * HEAD_SIZE)
    is_key = (jnp.arange(2 * HEAD_SIZE) < HEAD_SIZE)[None, None, None, :]
    spread = jnp.where(is_key, 2.0, 1.0)
    return (jnp.clip(jax.random.normal(key, complete_shape, jnp.float32), -4.0, 4.0) * spread).astype(jnp.bfloat16)


def plant(array, key, low, largest):
    spot = [jax.random.randint(jax.random.fold_in(key, axis), (), 0, length) for axis, length in enumerate(array.shape)]
    longest = array.shape.index(max(array.shape))
    next_to = spot[:longest] + [(spot[longest] + 1) % array.shape[longest]] + spot[longest + 1:]
    return array.at[tuple(spot)].set(low).at[tuple(next_to)].set(largest)


def block_levels(rng, shape, cuts, low, largest):
    factor_of, own = 1.0, jax.random.fold_in(rng, 6)
    for dim, parts in cuts:
        steps = jnp.exp(jax.random.uniform(jax.random.fold_in(own, dim), (parts,), jnp.float32, low / len(cuts), largest / len(cuts)))
        factor_of = factor_of * jnp.repeat(steps, shape[dim] // parts).reshape([-1 if axis == dim else 1 for axis in range(len(shape))])
    return factor_of


def assign_block(rng, own, number, rows, count, top, reach, slope):
    order = jax.random.permutation(rng, count)
    heavy_load, ordinary = load_shares(count, rows * top, reach, slope, True), load_shares(count, rows * top, reach, slope, False)
    places = jnp.arange(count)

    def named(tallies, turn):
        used = int((tallies > 0).sum())
        fixed = max(1, used // 4)
        shifted = fixed + (places - fixed + turn * (used - fixed)) % max(1, count - fixed)
        return jnp.zeros((count,), jnp.int32).at[order[jnp.where(places < fixed, places, shifted)]].set(jnp.asarray(tallies, jnp.int32))

    tallies = jnp.where(number % 4 == 0, named(heavy_load, number // 4), named(ordinary, number - number // 4 - 1))
    mixed = jax.random.permutation(jax.random.fold_in(own, 3), count)
    source_of, taker = mixed[0:count // 2 * 2:2], mixed[1:count // 2 * 2:2]
    slack = jnp.minimum(tallies[source_of] - 1, reach - tallies[taker]) // 2
    slack = jnp.where((source_of == order[0]) | (taker == order[0]) | (tallies[taker] == 0), 0, jnp.maximum(slack, 0))
    shifted = jax.random.randint(jax.random.fold_in(own, 4), (count // 2,), 0, 1 << 20) % (slack + 1)
    tallies = tallies.at[source_of].add(-shifted).at[taker].add(shifted)
    items = jnp.searchsorted(jnp.cumsum(tallies), jnp.arange(rows * top), side="right").astype(jnp.int32)
    table = items.reshape(top, rows).T
    table = table[jax.random.permutation(jax.random.fold_in(own, 1), rows)]
    turn = jax.random.randint(jax.random.fold_in(own, 2), (rows, 1), 0, top)
    return jnp.take_along_axis(table, (jnp.arange(top)[None, :] + turn) % top, axis=1)


def load_shares(count, total, bound, skew, full):
    portions = [(1 << 20) // math.isqrt(grade ** skew) + 1 for grade in range(1, count + 1)]
    largest = bound if full else min(bound, max(-(-total // count), total * portions[0] // sum(portions)))
    least = 1 if total - largest >= count - 1 else 0
    holding, spare = [largest] + [least] * (count - 1), total - largest - least * (count - 1)
    while spare > 0:
        candidates = [i for i in range(1, count) if holding[i] < largest] or [i for i in range(1, count) if holding[i] < bound]
        mass, budget = sum([portions[i] for i in candidates]), spare
        for i in candidates:
            extra = min(bound - holding[i], max(1, budget * portions[i] // mass), spare)
            holding[i] = holding[i] + extra
            spare = spare - extra
    return np.array(holding)


def centred(key, dims, scale, reach, cuts=(), kind=jnp.bfloat16):
    level = block_levels(key, dims, cuts, -0.22, 0.18) if cuts else 1.0
    entries = jax.random.normal(key, dims, jnp.float32) * scale * level
    return jnp.minimum(jnp.maximum(entries, -reach), reach).astype(kind)


def setup_inputs(seed: int = 0) -> dict:
    streams_of = jax.random.split(jax.random.key(seed), 14)
    hidden = centred(streams_of[0], (REQUEST_TOTAL, MODEL_DIM), 1.0, 6.0, ((0, 64), (1, 4)))
    lengths = draw_lengths(jax.random.fold_in(streams_of[13], 71), 0)
    migrate = plant(jax.random.randint(streams_of[2], (N_REQ,), 0, RQ_DEV), jax.random.fold_in(streams_of[2], 1), 0, RQ_DEV - 1).astype(jnp.int32)
    kv_cache = draw_kv_cache(jax.random.fold_in(streams_of[13], 71), 0)
    attn_gain = jnp.clip(1.0 + 0.18 * jax.random.normal(streams_of[4], (MODEL_DIM,), jnp.float32), 0.1, 1.9)
    moe_gain = jnp.clip(1.0 + 0.18 * jax.random.normal(streams_of[5], (MODEL_DIM,), jnp.float32), 0.1, 1.9)
    w_query = centred(streams_of[6], (MODEL_DIM, QUERY_HEADS * HEAD_SIZE), MODEL_DIM ** -0.5, 0.15625, ((1, 4),))
    key_value_weight = centred(streams_of[7], (MODEL_DIM, KEY_VALUE_HEADS * 2 * HEAD_SIZE), MODEL_DIM ** -0.5, 0.15625, ((1, 4),))
    output_weight = centred(streams_of[8], (QUERY_HEADS * HEAD_SIZE, MODEL_DIM), (KEY_VALUE_HEADS * HEAD_SIZE) ** -0.5, 0.25, ((0, 4),))
    w_gateup = centred(streams_of[9], (EXPERTS, MODEL_DIM, 2, EXP_HID), MODEL_DIM ** -0.5, 0.15625, ((0, 64), (3, 4)))
    w_down = centred(streams_of[10], (EXPERTS, EXP_HID, MODEL_DIM), EXP_HID ** -0.5, 0.25, ((0, 64), (1, 4)))
    expert_ids_keys = jax.random.split(jax.random.fold_in(streams_of[11], 1), REQUEST_TOTAL // RQ_DEV)
    expert_ids_turns = jax.random.permutation(jax.random.fold_in(streams_of[11], 3), REQUEST_TOTAL // RQ_DEV)
    expert_ids = jax.vmap(lambda own, number: assign_block(jax.random.fold_in(streams_of[11], 2), own, number, RQ_DEV, EXPERTS, TOPK, CAP, 2))(expert_ids_keys, expert_ids_turns).reshape((REQUEST_TOTAL, TOPK))
    expert_gates = jnp.clip(0.1 + 0.3 * jax.random.uniform(streams_of[12], (REQUEST_TOTAL, TOPK), jnp.float32) ** block_levels(streams_of[12], (REQUEST_TOTAL, TOPK), ((0, 64),), -0.2, 0.2), 0.1, 0.4)
    return dict(hidden=hidden, lengths=lengths, migrate=migrate, kv_cache=kv_cache, attn_gain=attn_gain, moe_gain=moe_gain, w_query=w_query, key_value_weight=key_value_weight, output_weight=output_weight, w_gateup=w_gateup, w_down=w_down, expert_ids=expert_ids, expert_gates=expert_gates)


epsilon = 1e-06
rope_base = 10000.0
masked_score = -1e+30

def rms_norm(values, gain):
    mean_square = lax.optimization_barrier(jnp.mean(values * values, axis=-1, keepdims=True))
    return values * lax.rsqrt(mean_square + epsilon) * gain

def apply_rotation(values, position):
    half_width = values.shape[-1] // 2
    inv_freq = rope_base ** (-jnp.arange(half_width, dtype=jnp.float32) * 2.0 / values.shape[-1])
    angles = position.astype(jnp.float32)[:, None, None] * inv_freq
    cosine = jnp.cos(angles)
    sine_part = jnp.sin(angles)
    first_half = values[..., :half_width]
    second_half = values[..., half_width:]
    return jnp.concatenate([first_half * cosine - second_half * sine_part, second_half * cosine + first_half * sine_part], axis=-1)

def reference(hidden, lengths, migrate, kv_cache, attn_gain, moe_gain, w_query, key_value_weight, output_weight, w_gateup, w_down, expert_ids, expert_gates):
    per_replica = N_REQ * RQ_DEV
    row_index = jnp.arange(REQUEST_TOTAL, dtype=jnp.int32)
    replica = row_index // per_replica
    within = row_index % per_replica
    is_moved = within % RQ_DEV == migrate[within // RQ_DEV]
    source = jnp.where(is_moved, (1 - replica) * per_replica + within, row_index).astype(jnp.int32)
    tokens = hidden[source]
    request_extent = lengths.reshape(-1)[source]
    normalized_input = rms_norm(tokens.astype(jnp.float32), attn_gain).astype(jnp.bfloat16)
    query_vectors = jnp.dot(normalized_input, w_query, preferred_element_type=jnp.float32).reshape(REQUEST_TOTAL, QUERY_HEADS, HEAD_SIZE)
    key_value_rows = jnp.dot(normalized_input, key_value_weight, preferred_element_type=jnp.float32).reshape(REQUEST_TOTAL, KEY_VALUE_HEADS, 2 * HEAD_SIZE)
    query_vectors = apply_rotation(query_vectors, request_extent).astype(jnp.bfloat16).reshape(REQUEST_TOTAL, KEY_VALUE_HEADS, QUERY_HEADS // KEY_VALUE_HEADS, HEAD_SIZE)
    key_new = apply_rotation(key_value_rows[..., :HEAD_SIZE], request_extent).astype(jnp.bfloat16)
    value_new = key_value_rows[..., HEAD_SIZE:].astype(jnp.bfloat16)
    score_scale = HEAD_SIZE ** (-0.5)

    def attend(request):
        anchor, query_row, key_row, value_row, span_now = request
        kv_rows = lax.dynamic_index_in_dim(kv_cache, anchor, 0, keepdims=False).astype(jnp.float32)
        cache_keys = kv_rows[..., :HEAD_SIZE]
        cache_values = kv_rows[..., HEAD_SIZE:]
        query_float = query_row.astype(jnp.float32)
        scores = jnp.einsum('hgd,thd->hgt', query_float, cache_keys) * score_scale
        own_score = jnp.einsum('hgd,hd->hg', query_float, key_row.astype(jnp.float32)) * score_scale
        visible = jnp.arange(CONTEXT_SLOTS, dtype=jnp.int32) < span_now
        scores = jnp.where(visible[None, None, :], scores, masked_score)
        row_peak = jnp.maximum(lax.optimization_barrier(jnp.max(scores, axis=-1)), own_score)
        cache_prob = jnp.exp(scores - row_peak[..., None])
        own_prob = jnp.exp(own_score - row_peak)
        denominator = lax.optimization_barrier(jnp.sum(cache_prob, axis=-1)) + own_prob
        cache_weight = lax.optimization_barrier((cache_prob / denominator[..., None]).astype(jnp.bfloat16)).astype(jnp.float32)
        own_weight = lax.optimization_barrier((own_prob / denominator).astype(jnp.bfloat16)).astype(jnp.float32)
        mixture = jnp.einsum('hgt,thd->hgd', cache_weight, cache_values)
        mixture = mixture + own_weight[..., None] * value_row.astype(jnp.float32)[:, None, :]
        return mixture.reshape(QUERY_HEADS * HEAD_SIZE)
    context = lax.map(attend, (source, query_vectors, key_new, value_new, request_extent)).astype(jnp.bfloat16)
    residual = tokens.astype(jnp.float32) + jnp.dot(context, output_weight, preferred_element_type=jnp.float32)
    expert_in = rms_norm(residual, moe_gain).astype(jnp.bfloat16)
    gate_weights = jnp.zeros((REQUEST_TOTAL, EXPERTS), jnp.float32).at[row_index[:, None], expert_ids].add(expert_gates)
    member_count = min(REQUEST_TOTAL, EXPERTS * CAP)

    def expert_step(mixture, expert):
        gate_up, down_rows, gate_column, expert_number = expert
        member = jnp.any(expert_ids == expert_number, axis=1).astype(jnp.int32)
        chosen = jnp.argsort(1 - member, stable=True)[:member_count].astype(jnp.int32)
        projected = jnp.dot(expert_in[chosen], gate_up.reshape(MODEL_DIM, 2 * EXP_HID), preferred_element_type=jnp.float32)
        activation = (jax.nn.silu(projected[:, :EXP_HID]) * projected[:, EXP_HID:]).astype(jnp.bfloat16)
        expert_out = jnp.dot(activation, down_rows, preferred_element_type=jnp.float32)
        return (mixture.at[chosen].add(gate_column[chosen][:, None] * expert_out), None)
    mixture, unused = lax.scan(expert_step, jnp.zeros((REQUEST_TOTAL, MODEL_DIM), jnp.float32), (w_gateup, w_down, gate_weights.T, jnp.arange(EXPERTS, dtype=jnp.int32)))
    return (residual + mixture).astype(jnp.bfloat16)
```

```python
import functools
import jax
import jax.numpy as jnp
import numpy as np
from jax import lax
from jax.experimental import pallas as pl
from jax.experimental.pallas import tpu as pltpu
from jax.sharding import PartitionSpec as P

MESH = pl.DeviceIdType.MESH
HEAD_SIZE = 64
EPSILON = 1e-06
ROPE_BASE = 10000.0
MASKED = -1e30
GATE_LANES = 128


def rows_of(scalars, n):
    row = lax.broadcasted_iota(jnp.int32, (n, 128), 0)
    out = jnp.zeros((n, 128), jnp.int32)
    for r in range(n):
        out = jnp.where(row == r, scalars(r), out)
    return out


def attend(q, kvn, kv, bias, limit):
    scale = HEAD_SIZE ** (-0.5)
    s = lax.dot_general(q.astype(jnp.bfloat16), kv, (((1,), (1,)), ((), ())), preferred_element_type=jnp.float32)
    lane = lax.broadcasted_iota(jnp.int32, s.shape, 1)
    s = jnp.where(lane < limit, s * scale + bias, MASKED)
    own = jnp.sum(q * kvn, axis=1, keepdims=True) * scale
    peak = jnp.maximum(jnp.max(s, axis=1, keepdims=True), own)
    p = jnp.exp(s - peak)
    p_own = jnp.exp(own - peak)
    inv = 1.0 / (jnp.sum(p, axis=1, keepdims=True) + p_own)
    w = (p * inv).astype(jnp.bfloat16)
    w_own = (p_own * inv).astype(jnp.bfloat16).astype(jnp.float32)
    return jnp.dot(w, kv, preferred_element_type=jnp.float32) + w_own * kvn


def attention_kernel(
    n_tp,
    len_s, mig_s, hid, kv_h, ag, mg, freq, wq_h, wkv_h, wo_h, ids, gates,
    x_out, res_out,
    kv_v, wq_v, wkv_v, wo_v, tok, kv_send, kv_recv, part_send, part_recv, q_s, kvn_s, ctx_s, bias_s,
    load_sem, kv_sem, tok_send_sem, tok_recv_sem, kv_send_sem, kv_recv_sem, part_send_sem, part_recv_sem,
):
    rep, tp = lax.axis_index("rep"), lax.axis_index("tp")
    n, width = hid.shape
    model = n_tp * width
    heads = wq_v.shape[1] // HEAD_SIZE
    kvh = wkv_v.shape[1] // (2 * HEAD_SIZE)
    group = heads // kvh
    n_lanes = kv_v.shape[1]

    loads = []
    for i, (src, dst) in enumerate(((wq_h, wq_v), (wkv_h, wkv_v))):
        loads.append(pltpu.make_async_copy(src, dst, load_sem.at[i]))
    load_o = pltpu.make_async_copy(wo_h, wo_v, load_sem.at[2])
    for c in loads:
        c.start()
    kv_loads = [pltpu.make_async_copy(kv_h.at[r], kv_v.at[r], kv_sem.at[r]) for r in range(n)]
    for c in kv_loads:
        c.start()
    load_o.start()

    barrier = pltpu.get_barrier_semaphore()
    peers = []
    for k in range(1, n_tp):
        peers.append((0, lax.rem(tp + k, n_tp)))
    for k in range(n_tp):
        peers.append((1, lax.rem(tp + k, n_tp)))
    for side, t in peers:
        r = rep if side == 0 else 1 - rep
        pl.semaphore_signal(barrier, inc=1, device_id={"rep": r, "tp": t}, device_id_type=MESH)
    pl.semaphore_wait(barrier, len(peers))

    sends = []
    for i, (side, t) in enumerate(peers):
        r = rep if side == 0 else 1 - rep
        c = pltpu.make_async_remote_copy(
            src_ref=hid, dst_ref=tok.at[side, tp], send_sem=tok_send_sem.at[i],
            recv_sem=tok_recv_sem.at[side, tp], device_id={"rep": r, "tp": t}, device_id_type=MESH)
        c.start()
        sends.append(c)
    tok[0, tp] = hid[...]

    slot = mig_s[0]
    row = lax.broadcasted_iota(jnp.int32, (n, 128), 0)
    lane = lax.broadcasted_iota(jnp.int32, (n, 128), 1)
    moved = row == slot
    own_span = rows_of(lambda r: jnp.where(rep == 0, len_s[0, r], len_s[1, r]), n)
    other_span = rows_of(lambda r: jnp.where(rep == 0, len_s[1, r], len_s[0, r]), n)
    span = jnp.where(moved, other_span, own_span).astype(jnp.float32)
    angle = span * freq[...]
    cosine, sine = jnp.cos(angle), jnp.sin(angle)
    first = lax.rem(lane, HEAD_SIZE) < HEAD_SIZE // 2
    half = HEAD_SIZE // 2

    def rotate(v):
        turned = jnp.where(first, -pltpu.roll(v, 128 - half, 1), pltpu.roll(v, half, 1))
        return v * cosine + turned * sine

    head = lax.broadcasted_iota(jnp.int32, (8, n_lanes), 0)
    pos = lax.broadcasted_iota(jnp.int32, (8, n_lanes), 1)
    bias_s[...] = jnp.where(lax.rem(pos, kvh) == head // group, 0.0, MASKED)

    eye = row == lane
    expert = lax.rem(lane, GATE_LANES // 2)
    dense = jnp.zeros((n, 128), jnp.float32)
    for k in range(ids.shape[0]):
        idc = jnp.sum(jnp.where(eye, ids[k:k + 1, :], 0), axis=1, keepdims=True)
        gc = jnp.sum(jnp.where(eye, gates[k:k + 1, :], 0.0), axis=1, keepdims=True)
        dense = dense + jnp.where(expert == idc, gc, 0.0)
    high = dense.astype(jnp.bfloat16)
    low = (dense - high.astype(jnp.float32)).astype(jnp.bfloat16)
    x_out[:, 0:GATE_LANES] = jnp.where(lane < GATE_LANES // 2, high.astype(jnp.float32), low.astype(jnp.float32)).astype(jnp.bfloat16)

    for side, t in peers:
        pltpu.make_async_remote_copy(
            src_ref=hid, dst_ref=tok.at[side, t], send_sem=tok_send_sem.at[0],
            recv_sem=tok_recv_sem.at[side, t], device_id={"tp": t}, device_id_type=MESH).wait_recv()
    for c in sends:
        c.wait_send()

    moved_w = lax.broadcasted_iota(jnp.int32, (n, width), 0) == slot
    tokens = jnp.concatenate(
        [jnp.where(moved_w, tok[1, t].astype(jnp.float32), tok[0, t].astype(jnp.float32)) for t in range(n_tp)], axis=1)
    mean = jnp.mean(tokens * tokens, axis=1, keepdims=True)
    normed = (tokens * lax.rsqrt(mean + EPSILON) * ag[...]).astype(jnp.bfloat16)
    for c in loads:
        c.wait()
    queries = jnp.dot(normed, wq_v[...], preferred_element_type=jnp.float32)
    keyval = jnp.dot(normed, wkv_v[...], preferred_element_type=jnp.float32)
    q_s[...] = jnp.zeros_like(q_s)
    kvn_s[...] = jnp.zeros_like(kvn_s)
    low_lanes = lane < HEAD_SIZE
    for b in range(heads // 2):
        turned = rotate(queries[:, b * 128:(b + 1) * 128]).astype(jnp.bfloat16).astype(jnp.float32)
        q_s[:, 2 * b, :] = jnp.where(low_lanes, turned, 0.0)
        q_s[:, 2 * b + 1, :] = jnp.where(low_lanes, pltpu.roll(turned, HEAD_SIZE, 1), 0.0)
    for g in range(kvh):
        both = keyval[:, g * 128:(g + 1) * 128]
        both = jnp.where(low_lanes, rotate(both), both).astype(jnp.bfloat16).astype(jnp.float32)
        for h in range(g * group, (g + 1) * group):
            kvn_s[:, h, :] = both

    for c in kv_loads:
        c.wait()
    kv_send[...] = kv_v[slot]
    kv_copy = pltpu.make_async_remote_copy(
        src_ref=kv_send, dst_ref=kv_recv, send_sem=kv_send_sem, recv_sem=kv_recv_sem,
        device_id={"rep": 1 - rep}, device_id_type=MESH)
    kv_copy.start()

    def one(r):
        limit = kvh * jnp.where(rep == 0, len_s[0, r], len_s[1, r])
        ctx_s[r] = attend(q_s[r], kvn_s[r], kv_v[r], bias_s[...], limit)

    UNROLL = 4

    def step(i, carry):
        for j in range(UNROLL):
            one(i * UNROLL + j)
        return carry

    lax.fori_loop(0, n // UNROLL, step, 0)
    kv_copy.wait()
    limit = kvh * jnp.where(rep == 0, len_s[1, slot], len_s[0, slot])
    arrived = attend(q_s[slot], kvn_s[slot], kv_recv[...], bias_s[...], limit)

    blocks = []
    for b in range(heads // 2):
        even = jnp.where(moved, arrived[2 * b:2 * b + 1], ctx_s[:, 2 * b, :])
        odd = jnp.where(moved, arrived[2 * b + 1:2 * b + 2], ctx_s[:, 2 * b + 1, :])
        blocks.append(jnp.where(low_lanes, pltpu.roll(even, HEAD_SIZE, 1), odd))
    context = jnp.concatenate(blocks, axis=1).astype(jnp.bfloat16)
    load_o.wait()
    partial = jnp.dot(context, wo_v[...], preferred_element_type=jnp.float32)
    part_send[...] = partial.astype(jnp.bfloat16)
    sends = []
    for k in range(1, n_tp):
        t = lax.rem(tp + k, n_tp)
        c = pltpu.make_async_remote_copy(
            src_ref=part_send, dst_ref=part_recv.at[tp], send_sem=part_send_sem.at[k],
            recv_sem=part_recv_sem.at[tp], device_id={"tp": t}, device_id_type=MESH)
        c.start()
        sends.append(c)
    total = tokens + part_send[...].astype(jnp.float32)
    for k in range(1, n_tp):
        t = lax.rem(tp + k, n_tp)
        pltpu.make_async_remote_copy(
            src_ref=part_send, dst_ref=part_recv.at[t], send_sem=part_send_sem.at[k],
            recv_sem=part_recv_sem.at[t], device_id={"tp": t}, device_id_type=MESH).wait_recv()
        total = total + part_recv[t].astype(jnp.float32)
    mean = jnp.mean(total * total, axis=1, keepdims=True)
    x_out[:, GATE_LANES:] = (total * lax.rsqrt(mean + EPSILON) * mg[...]).astype(jnp.bfloat16)
    mine = jnp.zeros((n, width), jnp.float32)
    for t in range(n_tp):
        mine = jnp.where(tp == t, total[:, t * width:(t + 1) * width], mine)
    res_out[...] = mine
    for c in sends:
        c.wait_send()


def attention(n_tp, lengths, migrate, hidden, kv_cache, attn_gain, moe_gain, w_query, key_value_weight, output_weight, expert_ids, expert_gates):
    n, width = hidden.shape
    model = w_query.shape[0]
    kvh = kv_cache.shape[2]
    kv = kv_cache.reshape(n, kv_cache.shape[1] * kvh, kv_cache.shape[3])
    lanes = kv.shape[1]
    i = np.arange(128) % (HEAD_SIZE // 2)
    freq = jnp.asarray((ROPE_BASE ** (-2.0 * i / HEAD_SIZE)).astype(np.float32)[None])
    ids = jnp.pad(expert_ids.T, ((0, 0), (0, 128 - n)))
    gates = jnp.pad(expert_gates.T, ((0, 0), (0, 128 - n)))
    smem, vmem, hbm = (pl.BlockSpec(memory_space=s) for s in (pltpu.SMEM, pltpu.VMEM, pl.ANY))
    bf, f32 = jnp.bfloat16, jnp.float32
    dma = pltpu.SemaphoreType.DMA
    return pl.pallas_call(
        functools.partial(attention_kernel, n_tp),
        name="attention",
        out_shape=(jax.ShapeDtypeStruct((n, GATE_LANES + model), bf), jax.ShapeDtypeStruct((n, width), f32)),
        in_specs=[smem, smem, vmem, hbm, vmem, vmem, vmem, hbm, hbm, hbm, vmem, vmem],
        out_specs=(vmem, vmem),
        scratch_shapes=[
            pltpu.VMEM(kv.shape, bf),
            pltpu.VMEM(w_query.shape, bf), pltpu.VMEM(key_value_weight.shape, bf), pltpu.VMEM(output_weight.shape, bf),
            pltpu.VMEM((2, n_tp, n, width), bf),
            pltpu.VMEM(kv.shape[1:], bf), pltpu.VMEM(kv.shape[1:], bf),
            pltpu.VMEM((n, model), bf), pltpu.VMEM((n_tp, n, model), bf),
            pltpu.VMEM((n, 8, 128), f32), pltpu.VMEM((n, 8, 128), f32), pltpu.VMEM((n, 8, 128), f32),
            pltpu.VMEM((8, lanes), f32),
            dma((3,)), dma((n,)), dma((2 * n_tp,)), dma((2, n_tp)), dma, dma, dma((n_tp,)), dma((n_tp,)),
        ],
        compiler_params=pltpu.CompilerParams(collective_id=0, has_side_effects=True, vmem_limit_bytes=50 * 2**20),
        cost_estimate=pl.CostEstimate(flops=200_000_000, bytes_accessed=12_000_000, transcendentals=1_000_000),
    )(lengths, migrate, hidden, kv, attn_gain.reshape(1, -1), moe_gain.reshape(1, -1), freq, w_query, key_value_weight, output_weight, ids, gates)


def shards(
    hidden,
    lengths,
    migrate,
    kv_cache,
    attn_gain,
    moe_gain,
    w_query,
    key_value_weight,
    output_weight,
    w_gateup,
    w_down,
    expert_ids,
    expert_gates,
):
    row_count = hidden.shape[0]
    x, own_residual = attention(lax.axis_size('tp'), lengths, migrate, hidden, kv_cache, attn_gain, moe_gain, w_query, key_value_weight, output_weight, expert_ids, expert_gates)
    expert_in = x[:, GATE_LANES:]
    expert_count = lax.axis_size("rep") * lax.axis_size("req")
    top_count = expert_ids.shape[1]
    capacity = min(row_count, max(3, 3 * row_count * top_count // expert_count))
    flat_ids = expert_ids.reshape(-1)
    matches = (flat_ids[:, None] == jnp.arange(expert_count, dtype=jnp.int32)[None, :]).astype(
        jnp.int32
    )
    slot_rank = jnp.sum((jnp.cumsum(matches, axis=0) - matches) * matches, axis=1)
    slot_target = flat_ids * capacity + slot_rank
    slot_table = (
        slot_target[:, None] == jnp.arange(expert_count * capacity, dtype=jnp.int32)[None, :]
    ).astype(jnp.float32)
    route_table = slot_table.reshape(row_count, top_count, -1).sum(axis=1)
    gate_table = (
        (slot_table * expert_gates.reshape(-1, 1)).reshape(row_count, top_count, -1).sum(axis=1)
    )
    outbound = jnp.einsum(
        "rs,rd->sd", route_table.astype(jnp.bfloat16), expert_in, preferred_element_type=jnp.float32
    ).astype(jnp.bfloat16)
    outbound = outbound.reshape(expert_count, capacity, -1)
    gate_up = w_gateup[0].reshape(w_gateup.shape[1], -1)
    down_rows = w_down[0]
    arrived_rows = lax.all_to_all(outbound, ("rep", "req"), split_axis=0, concat_axis=0, tiled=True)
    model_width = arrived_rows.shape[2]
    flattened = arrived_rows.reshape(-1, model_width)
    projected = jnp.dot(flattened, gate_up, preferred_element_type=jnp.float32)
    split_at = projected.shape[1] // 2
    activation = (jax.nn.silu(projected[:, :split_at]) * projected[:, split_at:]).astype(
        jnp.bfloat16
    )
    expert_part = jnp.dot(activation, down_rows, preferred_element_type=jnp.float32)
    expert_part = expert_part.reshape(arrived_rows.shape[0], arrived_rows.shape[1], model_width)
    returned = lax.all_to_all(
        expert_part.astype(jnp.bfloat16), ("rep", "req"), split_axis=0, concat_axis=0, tiled=True
    ).astype(expert_part.dtype)
    returned_rows = returned.reshape(expert_count * capacity, -1)
    combined = jnp.dot(
        gate_table,
        returned_rows,
        precision=lax.Precision.HIGHEST,
        preferred_element_type=jnp.float32,
    )
    expert_mix = lax.psum_scatter(
        combined.astype(jnp.bfloat16), "tp", scatter_dimension=1, tiled=True
    ).astype(jnp.float32)
    return (own_residual + expert_mix).astype(jnp.bfloat16)


def solution(mesh):
    placed = (
        P(("rep", "req"), "tp"),
        P(None, "req"),
        P("req"),
        P(("rep", "req"), None, "tp", None),
        P(),
        P(),
        P(None, "tp"),
        P(None, "tp"),
        P("tp", None),
        P(("rep", "req"), None, None, "tp"),
        P(("rep", "req"), "tp", None),
        P(("rep", "req"), None),
        P(("rep", "req"), None),
    )
    return jax.shard_map(
        shards, mesh=mesh, in_specs=placed, out_specs=P(("rep", "req"), "tp"), check_vma=False
    )
```

```python
import functools
import jax
import jax.numpy as jnp
import numpy as np
from jax import lax
from jax.experimental import pallas as pl
from jax.experimental.pallas import tpu as pltpu
from jax.sharding import PartitionSpec as P

MESH = pl.DeviceIdType.MESH
HEAD_SIZE = 64
EPSILON = 1e-06
ROPE_BASE = 10000.0
MASKED = -1e30
GATE_LANES = 128


def rows_of(scalars, n):
    row = lax.broadcasted_iota(jnp.int32, (n, 128), 0)
    out = jnp.zeros((n, 128), jnp.int32)
    for r in range(n):
        out = jnp.where(row == r, scalars(r), out)
    return out


def attend(q, kvn, kv, bias, limit):
    scale = HEAD_SIZE ** (-0.5)
    s = lax.dot_general(q.astype(jnp.bfloat16), kv, (((1,), (1,)), ((), ())), preferred_element_type=jnp.float32)
    lane = lax.broadcasted_iota(jnp.int32, s.shape, 1)
    s = jnp.where(lane < limit, s * scale + bias, MASKED)
    own = jnp.sum(q * kvn, axis=1, keepdims=True) * scale
    peak = jnp.maximum(jnp.max(s, axis=1, keepdims=True), own)
    p = jnp.exp(s - peak)
    p_own = jnp.exp(own - peak)
    inv = 1.0 / (jnp.sum(p, axis=1, keepdims=True) + p_own)
    w = (p * inv).astype(jnp.bfloat16)
    w_own = (p_own * inv).astype(jnp.bfloat16).astype(jnp.float32)
    return jnp.dot(w, kv, preferred_element_type=jnp.float32) + w_own * kvn


def attention_kernel(
    n_tp,
    len_s, mig_s, hid, kv_h, ag, mg, freq, wq_h, wkv_h, wo_h, ids, gates,
    x_out, res_out,
    kv_v, wq_v, wkv_v, wo_v, tok, kv_send, kv_recv, part_send, part_recv, q_s, kvn_s, ctx_s, bias_s,
    load_sem, kv_sem, tok_send_sem, tok_recv_sem, kv_send_sem, kv_recv_sem, part_send_sem, part_recv_sem,
):
    rep, tp = lax.axis_index("rep"), lax.axis_index("tp")
    n, width = hid.shape
    model = n_tp * width
    heads = wq_v.shape[1] // HEAD_SIZE
    kvh = wkv_v.shape[1] // (2 * HEAD_SIZE)
    group = heads // kvh
    n_lanes = kv_v.shape[1]

    loads = []
    for i, (src, dst) in enumerate(((wq_h, wq_v), (wkv_h, wkv_v))):
        loads.append(pltpu.make_async_copy(src, dst, load_sem.at[i]))
    load_o = pltpu.make_async_copy(wo_h, wo_v, load_sem.at[2])
    for c in loads:
        c.start()
    kv_loads = [pltpu.make_async_copy(kv_h.at[r], kv_v.at[r], kv_sem.at[r]) for r in range(n)]
    for c in kv_loads:
        c.start()
    load_o.start()

    barrier = pltpu.get_barrier_semaphore()
    peers = []
    for k in range(1, n_tp):
        peers.append((0, lax.rem(tp + k, n_tp)))
    for k in range(n_tp):
        peers.append((1, lax.rem(tp + k, n_tp)))
    for side, t in peers:
        r = rep if side == 0 else 1 - rep
        pl.semaphore_signal(barrier, inc=1, device_id={"rep": r, "tp": t}, device_id_type=MESH)
    pl.semaphore_wait(barrier, len(peers))

    sends = []
    for i, (side, t) in enumerate(peers):
        r = rep if side == 0 else 1 - rep
        c = pltpu.make_async_remote_copy(
            src_ref=hid, dst_ref=tok.at[side, tp], send_sem=tok_send_sem.at[i],
            recv_sem=tok_recv_sem.at[side, tp], device_id={"rep": r, "tp": t}, device_id_type=MESH)
        c.start()
        sends.append(c)
    tok[0, tp] = hid[...]

    slot = mig_s[0]
    row = lax.broadcasted_iota(jnp.int32, (n, 128), 0)
    lane = lax.broadcasted_iota(jnp.int32, (n, 128), 1)
    moved = row == slot
    own_span = rows_of(lambda r: jnp.where(rep == 0, len_s[0, r], len_s[1, r]), n)
    other_span = rows_of(lambda r: jnp.where(rep == 0, len_s[1, r], len_s[0, r]), n)
    span = jnp.where(moved, other_span, own_span).astype(jnp.float32)
    angle = span * freq[...]
    cosine, sine = jnp.cos(angle), jnp.sin(angle)
    first = lax.rem(lane, HEAD_SIZE) < HEAD_SIZE // 2
    half = HEAD_SIZE // 2

    def rotate(v):
        turned = jnp.where(first, -pltpu.roll(v, 128 - half, 1), pltpu.roll(v, half, 1))
        return v * cosine + turned * sine

    head = lax.broadcasted_iota(jnp.int32, (8, n_lanes), 0)
    pos = lax.broadcasted_iota(jnp.int32, (8, n_lanes), 1)
    bias_s[...] = jnp.where(lax.rem(pos, kvh) == head // group, 0.0, MASKED)

    eye = row == lane
    expert = lax.rem(lane, GATE_LANES // 2)
    dense = jnp.zeros((n, 128), jnp.float32)
    for k in range(ids.shape[0]):
        idc = jnp.sum(jnp.where(eye, ids[k:k + 1, :], 0), axis=1, keepdims=True)
        gc = jnp.sum(jnp.where(eye, gates[k:k + 1, :], 0.0), axis=1, keepdims=True)
        dense = dense + jnp.where(expert == idc, gc, 0.0)
    high = dense.astype(jnp.bfloat16)
    low = (dense - high.astype(jnp.float32)).astype(jnp.bfloat16)
    x_out[:, 0:GATE_LANES] = jnp.where(lane < GATE_LANES // 2, high.astype(jnp.float32), low.astype(jnp.float32)).astype(jnp.bfloat16)

    for side, t in peers:
        pltpu.make_async_remote_copy(
            src_ref=hid, dst_ref=tok.at[side, t], send_sem=tok_send_sem.at[0],
            recv_sem=tok_recv_sem.at[side, t], device_id={"tp": t}, device_id_type=MESH).wait_recv()
    for c in sends:
        c.wait_send()

    moved_w = lax.broadcasted_iota(jnp.int32, (n, width), 0) == slot
    tokens = jnp.concatenate(
        [jnp.where(moved_w, tok[1, t].astype(jnp.float32), tok[0, t].astype(jnp.float32)) for t in range(n_tp)], axis=1)
    mean = jnp.mean(tokens * tokens, axis=1, keepdims=True)
    normed = (tokens * lax.rsqrt(mean + EPSILON) * ag[...]).astype(jnp.bfloat16)
    for c in loads:
        c.wait()
    queries = jnp.dot(normed, wq_v[...], preferred_element_type=jnp.float32)
    keyval = jnp.dot(normed, wkv_v[...], preferred_element_type=jnp.float32)
    q_s[...] = jnp.zeros_like(q_s)
    kvn_s[...] = jnp.zeros_like(kvn_s)
    low_lanes = lane < HEAD_SIZE
    for b in range(heads // 2):
        turned = rotate(queries[:, b * 128:(b + 1) * 128]).astype(jnp.bfloat16).astype(jnp.float32)
        q_s[:, 2 * b, :] = jnp.where(low_lanes, turned, 0.0)
        q_s[:, 2 * b + 1, :] = jnp.where(low_lanes, pltpu.roll(turned, HEAD_SIZE, 1), 0.0)
    for g in range(kvh):
        both = keyval[:, g * 128:(g + 1) * 128]
        both = jnp.where(low_lanes, rotate(both), both).astype(jnp.bfloat16).astype(jnp.float32)
        for h in range(g * group, (g + 1) * group):
            kvn_s[:, h, :] = both

    for c in kv_loads:
        c.wait()
    kv_send[...] = kv_v[slot]
    kv_copy = pltpu.make_async_remote_copy(
        src_ref=kv_send, dst_ref=kv_recv, send_sem=kv_send_sem, recv_sem=kv_recv_sem,
        device_id={"rep": 1 - rep}, device_id_type=MESH)
    kv_copy.start()

    def one(r):
        limit = kvh * jnp.where(rep == 0, len_s[0, r], len_s[1, r])
        ctx_s[r] = attend(q_s[r], kvn_s[r], kv_v[r], bias_s[...], limit)

    UNROLL = 4

    def step(i, carry):
        for j in range(UNROLL):
            one(i * UNROLL + j)
        return carry

    lax.fori_loop(0, n // UNROLL, step, 0)
    kv_copy.wait()
    limit = kvh * jnp.where(rep == 0, len_s[1, slot], len_s[0, slot])
    arrived = attend(q_s[slot], kvn_s[slot], kv_recv[...], bias_s[...], limit)

    blocks = []
    for b in range(heads // 2):
        even = jnp.where(moved, arrived[2 * b:2 * b + 1], ctx_s[:, 2 * b, :])
        odd = jnp.where(moved, arrived[2 * b + 1:2 * b + 2], ctx_s[:, 2 * b + 1, :])
        blocks.append(jnp.where(low_lanes, pltpu.roll(even, HEAD_SIZE, 1), odd))
    context = jnp.concatenate(blocks, axis=1).astype(jnp.bfloat16)
    load_o.wait()
    partial = jnp.dot(context, wo_v[...], preferred_element_type=jnp.float32)
    part_send[...] = partial.astype(jnp.bfloat16)
    sends = []
    for k in range(1, n_tp):
        t = lax.rem(tp + k, n_tp)
        c = pltpu.make_async_remote_copy(
            src_ref=part_send, dst_ref=part_recv.at[tp], send_sem=part_send_sem.at[k],
            recv_sem=part_recv_sem.at[tp], device_id={"tp": t}, device_id_type=MESH)
        c.start()
        sends.append(c)
    total = tokens + part_send[...].astype(jnp.float32)
    for k in range(1, n_tp):
        t = lax.rem(tp + k, n_tp)
        pltpu.make_async_remote_copy(
            src_ref=part_send, dst_ref=part_recv.at[t], send_sem=part_send_sem.at[k],
            recv_sem=part_recv_sem.at[t], device_id={"tp": t}, device_id_type=MESH).wait_recv()
        total = total + part_recv[t].astype(jnp.float32)
    mean = jnp.mean(total * total, axis=1, keepdims=True)
    x_out[:, GATE_LANES:] = (total * lax.rsqrt(mean + EPSILON) * mg[...]).astype(jnp.bfloat16)
    mine = jnp.zeros((n, width), jnp.float32)
    for t in range(n_tp):
        mine = jnp.where(tp == t, total[:, t * width:(t + 1) * width], mine)
    res_out[...] = mine
    for c in sends:
        c.wait_send()


def attention(n_tp, lengths, migrate, hidden, kv_cache, attn_gain, moe_gain, w_query, key_value_weight, output_weight, expert_ids, expert_gates):
    n, width = hidden.shape
    model = w_query.shape[0]
    kvh = kv_cache.shape[2]
    kv = kv_cache.reshape(n, kv_cache.shape[1] * kvh, kv_cache.shape[3])
    lanes = kv.shape[1]
    i = np.arange(128) % (HEAD_SIZE // 2)
    freq = jnp.asarray((ROPE_BASE ** (-2.0 * i / HEAD_SIZE)).astype(np.float32)[None])
    ids = jnp.pad(expert_ids.T, ((0, 0), (0, 128 - n)))
    gates = jnp.pad(expert_gates.T, ((0, 0), (0, 128 - n)))
    smem, vmem, hbm = (pl.BlockSpec(memory_space=s) for s in (pltpu.SMEM, pltpu.VMEM, pl.ANY))
    bf, f32 = jnp.bfloat16, jnp.float32
    dma = pltpu.SemaphoreType.DMA
    return pl.pallas_call(
        functools.partial(attention_kernel, n_tp),
        name="attention",
        out_shape=(jax.ShapeDtypeStruct((n, GATE_LANES + model), bf), jax.ShapeDtypeStruct((n, width), f32)),
        in_specs=[smem, smem, vmem, hbm, vmem, vmem, vmem, hbm, hbm, hbm, vmem, vmem],
        out_specs=(vmem, vmem),
        scratch_shapes=[
            pltpu.VMEM(kv.shape, bf),
            pltpu.VMEM(w_query.shape, bf), pltpu.VMEM(key_value_weight.shape, bf), pltpu.VMEM(output_weight.shape, bf),
            pltpu.VMEM((2, n_tp, n, width), bf),
            pltpu.VMEM(kv.shape[1:], bf), pltpu.VMEM(kv.shape[1:], bf),
            pltpu.VMEM((n, model), bf), pltpu.VMEM((n_tp, n, model), bf),
            pltpu.VMEM((n, 8, 128), f32), pltpu.VMEM((n, 8, 128), f32), pltpu.VMEM((n, 8, 128), f32),
            pltpu.VMEM((8, lanes), f32),
            dma((3,)), dma((n,)), dma((2 * n_tp,)), dma((2, n_tp)), dma, dma, dma((n_tp,)), dma((n_tp,)),
        ],
        compiler_params=pltpu.CompilerParams(collective_id=0, has_side_effects=True, vmem_limit_bytes=67_000_000),
        cost_estimate=pl.CostEstimate(flops=200_000_000, bytes_accessed=12_000_000, transcendentals=1_000_000),
    )(lengths, migrate, hidden, kv, attn_gain.reshape(1, -1), moe_gain.reshape(1, -1), freq, w_query, key_value_weight, output_weight, ids, gates)


NY, NZ = 4, 8


def experts_kernel(
    n_tp, n_req,
    x, res, gu_h, dn_h,
    out,
    ga, gb, pa, pb, raw, wide, gu, dn,
    by_s, by_r, sa, ra, sb, rb, ys, yr, xs, xr, xf,
    load_sem, wx_s, wx_r, a1_s, a1_r, a2_s, a2_r, b1_s, b1_r, b2_s, b2_r,
    rby_s, rby_r, rsa_s, rsa_r, rsb_s, rsb_r, ry_s, ry_r, rx_s, rx_r,
):
    rep, req, tp = lax.axis_index("rep"), lax.axis_index("req"), lax.axis_index("tp")
    y, z = req // NZ, lax.rem(req, NZ)
    n = x.shape[0]
    a, b = ga.shape[-1], gb.shape[-1]
    f = pa.shape[-1]
    opp = NZ // 2
    bf, f32 = jnp.bfloat16, jnp.float32

    def zc(k):
        return lax.rem(z + (k + NZ), NZ)

    def yc(k):
        return lax.rem(y + k, NY)

    def at(yy, zz):
        return {"req": yy * NZ + zz}

    nbr = (at(y, zc(1)), at(y, zc(-1)))
    pending = []

    def rcopy(src, dst, ssem, rsem, dev):
        return pltpu.make_async_remote_copy(src_ref=src, dst_ref=dst, send_sem=ssem, recv_sem=rsem, device_id=dev, device_id_type=MESH)

    def send(*args):
        c = rcopy(*args)
        c.start()
        pending.append(c)

    def took(dst, ssem, rsem, dev):
        rcopy(dst, dst, ssem, rsem, dev).wait_recv()

    own_gu = pltpu.make_async_copy(gu_h, raw.at[0], load_sem.at[0])
    own_dn = pltpu.make_async_copy(dn_h, dn.at[0], load_sem.at[1])
    own_gu.start()
    own_dn.start()

    barrier = pltpu.get_barrier_semaphore()
    greet = [at(yc(k), z) for k in range(1, NY)] + [nbr[0], nbr[1]]
    greet += [{"tp": lax.rem(tp + k, n_tp)} for k in range(1, n_tp)] + [{"rep": 1 - rep}]
    for dev in greet:
        pl.semaphore_signal(barrier, inc=1, device_id=dev, device_id_type=MESH)
    pl.semaphore_wait(barrier, len(greet))

    HALF = ((0, 1), (2, 3))
    xa, xb = x.at[:, 0:a], x.at[:, a:a + b]
    for k in range(1, NY):
        send(xa, ga.at[z, y], a1_s.at[k], a1_r.at[y], at(yc(k), z))
    for d in (0, 1):
        send(xb, gb.at[z, y], b1_s.at[d, 1], b1_r.at[d, 1], nbr[d])
    for d in (0, 1):
        send(xa, ga.at[z, y], a2_s.at[d, 1, y], a2_r.at[d, 1, y], nbr[d])
    for k in range(1, NY):
        send(xb, gb.at[z, y], b2_s.at[0, k], b2_r.at[z, y], at(yc(k), z))
    partner = {"rep": 1 - rep}
    send(gu_h, raw.at[1], wx_s.at[0], wx_r.at[0], partner)
    send(dn_h, dn.at[1], wx_s.at[1], wx_r.at[1], partner)
    ga[z, y] = x[:, 0:a]
    gb[z, y] = x[:, a:a + b]

    for k in range(1, NY):
        yb = yc(k)
        took(ga.at[z, yb], a1_s.at[k], a1_r.at[yb], at(yb, z))
        for d in (0, 1):
            send(ga.at[z, yb], ga.at[z, yb], a2_s.at[d, 1, yb], a2_r.at[d, 1, yb], nbr[d])

    part = wide.shape[0]

    def split(j):
        def step(i, carry):
            start = pl.multiple_of(i * part, part)
            wide[...] = raw[j, pl.ds(start, part), :].astype(f32)
            rows = pl.ds(pl.multiple_of(i * (part // 2), part // 2), part // 2)
            gu[j, rows, 0:128] = wide[pl.ds(0, part // 2, stride=2), :].astype(bf)
            gu[j, rows, 128:256] = wide[pl.ds(1, part // 2, stride=2), :].astype(bf)
            return carry
        lax.fori_loop(0, raw.shape[1] // part, step, 0)

    own_gu.wait()
    split(0)

    number = (rep * n_req + req, (1 - rep) * n_req + req)

    def compute(zs):
        m = len(zs) * NY * n
        rows_a = jnp.concatenate([ga[zz].reshape(NY * n, a) for zz in zs], axis=0)
        rows_b = jnp.concatenate([gb[zz].reshape(NY * n, b) for zz in zs], axis=0)
        table = rows_a[:, 0:GATE_LANES].astype(f32)
        expert = lax.rem(lax.broadcasted_iota(jnp.int32, table.shape, 1), GATE_LANES // 2)
        acts = []
        for j in (0, 1):
            weight = jnp.sum(jnp.where(expert == number[j], table, 0.0), axis=1, keepdims=True)
            cut = a - GATE_LANES
            pr = jnp.dot(rows_a[:, GATE_LANES:], gu[j, 0:cut, :], preferred_element_type=f32)
            pr = pr + jnp.dot(rows_b, gu[j, cut:cut + b, :], preferred_element_type=f32)
            g, u = pr[:, 0:128], pr[:, 128:256]
            acts.append((g / (1.0 + jnp.exp(-g)) * u * weight).astype(bf))
        o = jnp.dot(acts[0], dn[0], preferred_element_type=f32) + jnp.dot(acts[1], dn[1], preferred_element_type=f32)
        for i, zz in enumerate(zs):
            block = o[i * NY * n:(i + 1) * NY * n]
            pa[zz] = block[:, 0:f].reshape(NY, n, f)
            pb[zz] = block[:, f:2 * f].reshape(NY, n, f)
            by_s[zz] = block[:, f:2 * f].astype(bf).reshape(NY, n, f)
            for k in range(1, NY):
                send(by_s.at[zz, yc(k)], by_r.at[zz, y], rby_s.at[zz, k], rby_r.at[zz, y], at(yc(k), z))

    def took_b2(zz):
        for k in range(1, NY):
            took(gb.at[zz, yc(k)], b2_s.at[0, k], b2_r.at[zz, yc(k)], at(yc(k), z))

    h = b // 2
    for s in range(1, opp + 1):
        for d in (0, 1):
            zz = zc(-s) if d == 0 else zc(s)
            if s < opp:
                took(gb.at[zz, y], b1_s.at[d, s], b1_r.at[d, s], nbr[d])
                block = gb.at[zz, y] if s + 1 < opp else gb.at[zz, y, :, d * h:(d + 1) * h]
                send(block, block, b1_s.at[d, s + 1], b1_r.at[d, s + 1], nbr[d])
                for k in range(1, NY):
                    send(gb.at[zz, y], gb.at[zz, y], b2_s.at[2 * s - 1 + d, k], b2_r.at[zz, y], at(yc(k), z))
            else:
                block = gb.at[zz, y, :, d * h:(d + 1) * h]
                took(block, b1_s.at[d, s], b1_r.at[d, s], nbr[d])
                if d == 1:
                    for k in range(1, NY):
                        send(gb.at[zz, y], gb.at[zz, y], b2_s.at[2 * s - 1, k], b2_r.at[zz, y], at(yc(k), z))
        for d in (0, 1):
            zz = zc(-s) if d == 0 else zc(s)
            for yb in range(NY) if s < opp else HALF[d]:
                took(ga.at[zz, yb], a2_s.at[d, s, yb], a2_r.at[d, s, yb], nbr[d])
                if s + 1 < opp or (s + 1 == opp and yb in HALF[d]):
                    send(ga.at[zz, yb], ga.at[zz, yb], a2_s.at[d, s + 1, yb], a2_r.at[d, s + 1, yb], nbr[d])
        if s == 1:
            own_dn.wait()
            took(raw.at[1], wx_s.at[0], wx_r.at[0], partner)
            took(dn.at[1], wx_s.at[1], wx_r.at[1], partner)
            split(1)
            took_b2(z)
            compute([z])
        else:
            near = [zc(-(s - 1)), zc(s - 1)]
            for zz in near:
                took_b2(zz)
            compute(near)
    far = zc(opp)
    took_b2(far)
    compute([far])

    def a_send(d, k, yb, value):
        sa[d, k, yb] = value.astype(bf)
        send(sa.at[d, k, yb], ra.at[d, k, yb], rsa_s.at[d, k, yb], rsa_r.at[d, k, yb], nbr[d])

    def a_step(k):
        for d in (0, 1):
            zz = zc(k) if d == 0 else zc(-k)
            for yb in range(NY) if k < opp else HALF[d]:
                value = pa[zz, yb]
                if k < opp - 1 or (k == opp - 1 and yb in HALF[d]):
                    took(ra.at[d, k + 1, yb], rsa_s.at[d, k + 1, yb], rsa_r.at[d, k + 1, yb], nbr[d])
                    value = value + ra[d, k + 1, yb].astype(f32)
                a_send(d, k, yb, value)

    def b_own(zz):
        value = pb[zz, y]
        for k in range(1, NY):
            took(by_r.at[zz, yc(k)], rby_s.at[zz, k], rby_r.at[zz, yc(k)], at(yc(k), z))
            value = value + by_r[zz, yc(k)].astype(f32)
        return value

    e = f // 2

    def b_step(k):
        if k == opp:
            value = b_own(zc(k)).astype(bf)
            for d in (0, 1):
                sb[d, k, :, d * e:(d + 1) * e] = value[:, d * e:(d + 1) * e]
                send(sb.at[d, k, :, d * e:(d + 1) * e], rb.at[d, k, :, d * e:(d + 1) * e], rsb_s.at[d, k], rsb_r.at[d, k], nbr[d])
            return
        for d in (0, 1):
            value = b_own(zc(k) if d == 0 else zc(-k))
            if k == opp - 1:
                part = rb.at[d, k + 1, :, d * e:(d + 1) * e]
                took(part, rsb_s.at[d, k + 1], rsb_r.at[d, k + 1], nbr[d])
                added = value[:, d * e:(d + 1) * e] + rb[d, k + 1, :, d * e:(d + 1) * e].astype(f32)
                value = jnp.concatenate([added, value[:, e:]] if d == 0 else [value[:, :e], added], axis=1)
            else:
                took(rb.at[d, k + 1], rsb_s.at[d, k + 1], rsb_r.at[d, k + 1], nbr[d])
                value = value + rb[d, k + 1].astype(f32)
            sb[d, k] = value.astype(bf)
            send(sb.at[d, k], rb.at[d, k], rsb_s.at[d, k], rsb_r.at[d, k], nbr[d])

    a_step(4)
    a_step(3)
    b_step(4)
    a_step(2)
    b_step(3)
    a_step(1)
    b_step(2)
    total_a = None
    for k in (1, 2, 3, 0):
        yb = yc(k)
        value = pa[z, yb]
        for d in (0, 1):
            took(ra.at[d, 1, yb], rsa_s.at[d, 1, yb], rsa_r.at[d, 1, yb], nbr[d])
            value = value + ra[d, 1, yb].astype(f32)
        if k:
            ys[yb] = value.astype(bf)
            send(ys.at[yb], yr.at[y], ry_s.at[k], ry_r.at[y], at(yb, z))
        else:
            total_a = value
    b_step(1)
    total_b = b_own(z)
    for d in (0, 1):
        took(rb.at[d, 1], rsb_s.at[d, 1], rsb_r.at[d, 1], nbr[d])
        total_b = total_b + rb[d, 1].astype(f32)
    for k in range(1, NY):
        yb = yc(k)
        took(yr.at[yb], ry_s.at[k], ry_r.at[yb], at(yb, z))
        total_a = total_a + yr[yb].astype(f32)

    width = out.shape[1]
    total = jnp.concatenate([total_a, total_b], axis=1)
    for t in range(n_tp):
        quarter = total[:, t * width:(t + 1) * width]
        xf[t] = quarter
        xs[t] = quarter.astype(bf)
    for k in range(1, n_tp):
        t = lax.rem(tp + k, n_tp)
        send(xs.at[t], xr.at[tp], rx_s.at[k], rx_r.at[tp], {"tp": t})
    value = res[...] + xf[tp]
    for k in range(1, n_tp):
        t = lax.rem(tp + k, n_tp)
        took(xr.at[t], rx_s.at[k], rx_r.at[t], {"tp": t})
        value = value + xr[t].astype(f32)
    out[...] = value.astype(bf)
    for c in pending:
        c.wait_send()


def experts(n_tp, n_req, x, res, w_gateup, w_down):
    n, wide = x.shape
    width = res.shape[1]
    model = w_down.shape[2]
    a = GATE_LANES + model // 2
    b = model // 2
    f = model // 2
    gu = w_gateup.reshape(2 * model, w_gateup.shape[3])
    dn = w_down[0]
    vmem, hbm = pl.BlockSpec(memory_space=pltpu.VMEM), pl.BlockSpec(memory_space=pl.ANY)
    bf, f32 = jnp.bfloat16, jnp.float32
    dma = pltpu.SemaphoreType.DMA
    v = pltpu.VMEM
    k5 = NZ // 2 + 1
    return pl.pallas_call(
        functools.partial(experts_kernel, n_tp, n_req),
        name="experts",
        out_shape=jax.ShapeDtypeStruct((n, width), bf),
        in_specs=[vmem, vmem, hbm, hbm],
        out_specs=vmem,
        scratch_shapes=[
            v((NZ, NY, n, a), bf), v((NZ, NY, n, b), bf), v((NZ, NY, n, f), f32), v((NZ, NY, n, f), f32),
            v((2,) + gu.shape, bf), v((512, 128), f32), v((2, model, 256), bf), v((2,) + dn.shape, bf),
            v((NZ, NY, n, f), bf), v((NZ, NY, n, f), bf),
            v((2, k5, NY, n, f), bf), v((2, k5, NY, n, f), bf), v((2, k5, n, f), bf), v((2, k5, n, f), bf),
            v((NY, n, f), bf), v((NY, n, f), bf), v((n_tp, n, width), bf), v((n_tp, n, width), bf), v((n_tp, n, width), f32),
            dma((2,)), dma((2,)), dma((2,)), dma((NY,)), dma((NY,)), dma((2, k5, NY)), dma((2, k5, NY)), dma((2, k5)), dma((2, k5)),
            dma((NZ, NY)), dma((NZ, NY)),
            dma((NZ, NY)), dma((NZ, NY)), dma((2, k5, NY)), dma((2, k5, NY)), dma((2, k5)), dma((2, k5)), dma((NY,)), dma((NY,)),
            dma((n_tp,)), dma((n_tp,)),
        ],
        compiler_params=pltpu.CompilerParams(collective_id=1, has_side_effects=True, vmem_limit_bytes=67_000_000),
        cost_estimate=pl.CostEstimate(flops=1_300_000_000, bytes_accessed=4_000_000, transcendentals=200_000),
    )(x, res, gu, dn)


def shards(
    hidden,
    lengths,
    migrate,
    kv_cache,
    attn_gain,
    moe_gain,
    w_query,
    key_value_weight,
    output_weight,
    w_gateup,
    w_down,
    expert_ids,
    expert_gates,
):
    n_tp, n_req = lax.axis_size("tp"), lax.axis_size("req")
    x, res = attention(
        n_tp, lengths, migrate, hidden, kv_cache, attn_gain, moe_gain, w_query, key_value_weight, output_weight,
        expert_ids, expert_gates)
    return experts(n_tp, n_req, x, res, w_gateup, w_down)


def solution(mesh):
    placed = (
        P(("rep", "req"), "tp"),
        P(None, "req"),
        P("req"),
        P(("rep", "req"), None, "tp", None),
        P(),
        P(),
        P(None, "tp"),
        P(None, "tp"),
        P("tp", None),
        P(("rep", "req"), None, None, "tp"),
        P(("rep", "req"), "tp", None),
        P(("rep", "req"), None),
        P(("rep", "req"), None),
    )
    return jax.shard_map(
        shards, mesh=mesh, in_specs=placed, out_specs=P(("rep", "req"), "tp"), check_vma=False
    )
```

```python
import functools
import jax
import jax.numpy as jnp
import numpy as np
from jax import lax
from jax.experimental import pallas as pl
from jax.experimental.pallas import tpu as pltpu
from jax.sharding import PartitionSpec as P

MESH = pl.DeviceIdType.MESH
HEAD_SIZE = 64
EPSILON = 1e-06
ROPE_BASE = 10000.0
MASKED = -1e30
GATE_LANES = 128
NY, NZ = 4, 8
VMEM_LIMIT = 58 * 2**20


def rows_of(scalars, n):
    row = lax.broadcasted_iota(jnp.int32, (n, 128), 0)
    out = jnp.zeros((n, 128), jnp.int32)
    for r in range(n):
        out = jnp.where(row == r, scalars(r), out)
    return out


def attend(q, kvn, kv, bias, limit):
    scale = HEAD_SIZE ** (-0.5)
    s = lax.dot_general(q.astype(jnp.bfloat16), kv, (((1,), (1,)), ((), ())), preferred_element_type=jnp.float32)
    lane = lax.broadcasted_iota(jnp.int32, s.shape, 1)
    s = jnp.where(lane < limit, s * scale + bias, MASKED)
    own = jnp.sum(q * kvn, axis=1, keepdims=True) * scale
    peak = jnp.maximum(jnp.max(s, axis=1, keepdims=True), own)
    p = jnp.exp(s - peak)
    p_own = jnp.exp(own - peak)
    inv = 1.0 / (jnp.sum(p, axis=1, keepdims=True) + p_own)
    w = (p * inv).astype(jnp.bfloat16)
    w_own = (p_own * inv).astype(jnp.bfloat16).astype(jnp.float32)
    return jnp.dot(w, kv, preferred_element_type=jnp.float32) + w_own * kvn


def layer_kernel(
    n_tp, n_req,
    len_h, mig_s, hid_h, kv_h, ag_h, mg_h, freq_h, wq_h, wkv_h, wo_h, ids_h, gates_h, gu_h, dn_h,
    out,
    len_s, hid, ag, mg, freq, ids, gates,
    kv_v, wq_v, wkv_v, wo_v, tok, kv_send, kv_recv, part_send, part_recv, q_s, kvn_s, ctx_s, bias_s,
    ga, gb, pa, pb, raw, wide, gu, dn,
    by_s, by_r, sa, ra, sb, rb, ys, yr, xs, xr, xf,
    load_sem, kv_sem, tok_send_sem, tok_recv_sem, kv_send_sem, kv_recv_sem, part_send_sem, part_recv_sem,
    wx_s, wx_r, a1_s, a1_r, a2_s, a2_r, b1_s, b1_r, b2_s, b2_r,
    rby_s, rby_r, rsa_s, rsa_r, rsb_s, rsb_r, ry_s, ry_r, rx_s, rx_r,
):
    rep, req, tp = lax.axis_index("rep"), lax.axis_index("req"), lax.axis_index("tp")
    y, z = req // NZ, lax.rem(req, NZ)
    n, width = hid.shape
    heads = wq_v.shape[1] // HEAD_SIZE
    kvh = wkv_v.shape[1] // (2 * HEAD_SIZE)
    group = heads // kvh
    n_lanes = kv_v.shape[1]
    a, b, f = ga.shape[-1], gb.shape[-1], pa.shape[-1]
    opp = NZ // 2
    bf, f32 = jnp.bfloat16, jnp.float32

    def zc(k):
        return lax.rem(z + (k + NZ), NZ)

    def yc(k):
        return lax.rem(y + k, NY)

    def tc(k):
        return lax.rem(tp + k, n_tp)

    def at(yy, zz):
        return {"req": yy * NZ + zz}

    nbr = (at(y, zc(1)), at(y, zc(-1)))
    partner = {"rep": 1 - rep}
    pending = []

    def rcopy(src, dst, ssem, rsem, dev):
        return pltpu.make_async_remote_copy(src_ref=src, dst_ref=dst, send_sem=ssem, recv_sem=rsem, device_id=dev, device_id_type=MESH)

    def send(*args):
        c = rcopy(*args)
        c.start()
        pending.append(c)

    def took(dst, ssem, rsem, dev):
        rcopy(dst, dst, ssem, rsem, dev).wait_recv()

    loads = []

    def load(src, dst):
        c = pltpu.make_async_copy(src, dst, load_sem.at[len(loads)])
        c.start()
        loads.append(c)
        return c

    small = [load(*p) for p in ((hid_h, hid), (len_h, len_s), (ids_h, ids), (gates_h, gates), (freq_h, freq), (ag_h, ag), (mg_h, mg))]
    proj = [load(wq_h, wq_v), load(wkv_h, wkv_v)]
    kv_loads = [pltpu.make_async_copy(kv_h.at[r], kv_v.at[r], kv_sem.at[r]) for r in range(n)]
    for c in kv_loads:
        c.start()
    load_o = load(wo_h, wo_v)
    own_gu = load(gu_h, raw.at[0])
    own_dn = load(dn_h, dn.at[0])

    barrier = pltpu.get_barrier_semaphore()
    peers = [(0, tc(k)) for k in range(1, n_tp)] + [(1, tc(k)) for k in range(n_tp)]
    far_rep = lambda side: rep if side == 0 else 1 - rep
    greet = [{"rep": far_rep(side), "tp": t} for side, t in peers]
    greet += [at(yc(k), z) for k in range(1, NY)] + [nbr[0], nbr[1]]
    for dev in greet:
        pl.semaphore_signal(barrier, inc=1, device_id=dev, device_id_type=MESH)
    pl.semaphore_wait(barrier, len(greet))

    for c in small:
        c.wait()
    for i, (side, t) in enumerate(peers):
        send(hid, tok.at[side, tp], tok_send_sem.at[i], tok_recv_sem.at[side, tp], {"rep": far_rep(side), "tp": t})
    tok[0, tp] = hid[...]
    send(gu_h, raw.at[1], wx_s.at[0], wx_r.at[0], partner)
    send(dn_h, dn.at[1], wx_s.at[1], wx_r.at[1], partner)

    slot = mig_s[0]
    row = lax.broadcasted_iota(jnp.int32, (n, 128), 0)
    lane = lax.broadcasted_iota(jnp.int32, (n, 128), 1)
    moved = row == slot
    own_span = rows_of(lambda r: jnp.where(rep == 0, len_s[0, r], len_s[1, r]), n)
    other_span = rows_of(lambda r: jnp.where(rep == 0, len_s[1, r], len_s[0, r]), n)
    span = jnp.where(moved, other_span, own_span).astype(f32)
    angle = span * freq[...]
    cosine, sine = jnp.cos(angle), jnp.sin(angle)
    first = lax.rem(lane, HEAD_SIZE) < HEAD_SIZE // 2
    half = HEAD_SIZE // 2

    def rotate(v):
        turned = jnp.where(first, -pltpu.roll(v, 128 - half, 1), pltpu.roll(v, half, 1))
        return v * cosine + turned * sine

    head = lax.broadcasted_iota(jnp.int32, (8, n_lanes), 0)
    pos = lax.broadcasted_iota(jnp.int32, (8, n_lanes), 1)
    bias_s[...] = jnp.where(lax.rem(pos, kvh) == head // group, 0.0, MASKED)

    eye = lax.broadcasted_iota(jnp.int32, (n, n), 0) == lax.broadcasted_iota(jnp.int32, (n, n), 1)
    expert = lax.rem(lane, GATE_LANES // 2)
    dense = jnp.zeros((n, 128), f32)
    for k in range(ids.shape[0]):
        idc = jnp.sum(jnp.where(eye, ids[k:k + 1, :], 0), axis=1, keepdims=True)
        gc = jnp.sum(jnp.where(eye, gates[k:k + 1, :], 0.0), axis=1, keepdims=True)
        dense = dense + jnp.where(expert == idc, gc, 0.0)
    high = dense.astype(bf).astype(f32)
    ga[z, y, :, 0:GATE_LANES] = jnp.where(lane < GATE_LANES // 2, high, dense - high).astype(bf)

    part = wide.shape[0]

    def split(j):
        def step(i, carry):
            start = pl.multiple_of(i * part, part)
            wide[...] = raw[j, pl.ds(start, part), :].astype(f32)
            rows = pl.ds(pl.multiple_of(i * (part // 2), part // 2), part // 2)
            gu[j, rows, 0:128] = wide[pl.ds(0, part // 2, stride=2), :].astype(bf)
            gu[j, rows, 128:256] = wide[pl.ds(1, part // 2, stride=2), :].astype(bf)
            return carry
        lax.fori_loop(0, raw.shape[1] // part, step, 0)

    for side, t in peers:
        took(tok.at[side, t], tok_send_sem.at[0], tok_recv_sem.at[side, t], {"tp": t})

    moved_w = lax.broadcasted_iota(jnp.int32, (n, width), 0) == slot
    tokens = jnp.concatenate(
        [jnp.where(moved_w, tok[1, t].astype(f32), tok[0, t].astype(f32)) for t in range(n_tp)], axis=1)
    mean = jnp.mean(tokens * tokens, axis=1, keepdims=True)
    gain = jnp.concatenate([ag[i:i + 1, :] for i in range(ag.shape[0])], axis=1)
    normed = (tokens * lax.rsqrt(mean + EPSILON) * gain).astype(bf)
    for c in proj:
        c.wait()
    queries = jnp.dot(normed, wq_v[...], preferred_element_type=f32)
    keyval = jnp.dot(normed, wkv_v[...], preferred_element_type=f32)
    q_s[...] = jnp.zeros_like(q_s)
    kvn_s[...] = jnp.zeros_like(kvn_s)
    low_lanes = lane < HEAD_SIZE
    for i in range(heads // 2):
        turned = rotate(queries[:, i * 128:(i + 1) * 128]).astype(bf).astype(f32)
        q_s[:, 2 * i, :] = jnp.where(low_lanes, turned, 0.0)
        q_s[:, 2 * i + 1, :] = jnp.where(low_lanes, pltpu.roll(turned, HEAD_SIZE, 1), 0.0)
    for g in range(kvh):
        both = keyval[:, g * 128:(g + 1) * 128]
        both = jnp.where(low_lanes, rotate(both), both).astype(bf).astype(f32)
        for h in range(g * group, (g + 1) * group):
            kvn_s[:, h, :] = both

    for c in kv_loads:
        c.wait()
    kv_send[...] = kv_v[slot]
    kv_copy = rcopy(kv_send, kv_recv, kv_send_sem, kv_recv_sem, partner)
    kv_copy.start()

    def one(r):
        limit = kvh * jnp.where(rep == 0, len_s[0, r], len_s[1, r])
        ctx_s[r] = attend(q_s[r], kvn_s[r], kv_v[r], bias_s[...], limit)

    UNROLL = 4

    def step(i, carry):
        for j in range(UNROLL):
            one(i * UNROLL + j)
        return carry

    lax.fori_loop(0, n // UNROLL, step, 0)
    kv_copy.wait()
    limit = kvh * jnp.where(rep == 0, len_s[1, slot], len_s[0, slot])
    arrived = attend(q_s[slot], kvn_s[slot], kv_recv[...], bias_s[...], limit)

    blocks = []
    for i in range(heads // 2):
        even = jnp.where(moved, arrived[2 * i:2 * i + 1], ctx_s[:, 2 * i, :])
        odd = jnp.where(moved, arrived[2 * i + 1:2 * i + 2], ctx_s[:, 2 * i + 1, :])
        blocks.append(jnp.where(low_lanes, pltpu.roll(even, HEAD_SIZE, 1), odd))
    context = jnp.concatenate(blocks, axis=1).astype(bf)
    load_o.wait()
    partial = jnp.dot(context, wo_v[...], preferred_element_type=f32)
    part_send[...] = partial.astype(bf)
    for k in (1, 3, 2):
        send(part_send, part_recv.at[tp], part_send_sem.at[k], part_recv_sem.at[tp], {"tp": tc(k)})
    own_gu.wait()
    own_dn.wait()
    split(0)
    took(raw.at[1], wx_s.at[0], wx_r.at[0], partner)
    took(dn.at[1], wx_s.at[1], wx_r.at[1], partner)
    split(1)
    total = tokens + partial
    for k in (1, 3, 2):
        t = tc(k)
        took(part_recv.at[t], part_send_sem.at[k], part_recv_sem.at[t], {"tp": t})
        total = total + part_recv[t].astype(f32)
    mean = jnp.mean(total * total, axis=1, keepdims=True)
    gain = jnp.concatenate([mg[i:i + 1, :] for i in range(mg.shape[0])], axis=1)
    x = (total * lax.rsqrt(mean + EPSILON) * gain).astype(bf)
    cut = a - GATE_LANES
    ga[z, y, :, GATE_LANES:] = x[:, 0:cut]
    gb[z, y] = x[:, cut:]

    ORDER = (0, 1, 3, 2)
    REL = ((0, 1), (3, 2))
    AWAY = (1, 3, 2)
    for d in (0, 1):
        send(ga.at[z, y], ga.at[z, y], a2_s.at[d, 1, 0], a2_r.at[d, 1, 0], nbr[d])
    for k in AWAY:
        send(ga.at[z, y], ga.at[z, y], a1_s.at[k], a1_r.at[y], at(yc(k), z))
    for d in (0, 1):
        send(gb.at[z, y], gb.at[z, y], b1_s.at[d, 1], b1_r.at[d, 1], nbr[d])
    for k in AWAY:
        send(gb.at[z, y], gb.at[z, y], b2_s.at[0, k], b2_r.at[z, y], at(yc(k), z))
    own = jnp.zeros((n, width), f32)
    for t in range(n_tp):
        own = jnp.where(tp == t, total[:, t * width:(t + 1) * width], own)
    xf[n_tp] = own
    for k in AWAY:
        yb = yc(k)
        took(ga.at[z, yb], a1_s.at[k], a1_r.at[yb], at(yb, z))
        for d in (0, 1):
            send(ga.at[z, yb], ga.at[z, yb], a2_s.at[d, 1, k], a2_r.at[d, 1, k], nbr[d])

    number = (rep * n_req + req, (1 - rep) * n_req + req)

    def compute(zs):
        rows_a = jnp.concatenate([ga[zz].reshape(NY * n, a) for zz in zs], axis=0)
        rows_b = jnp.concatenate([gb[zz].reshape(NY * n, b) for zz in zs], axis=0)
        table = rows_a[:, 0:GATE_LANES].astype(f32)
        which = lax.rem(lax.broadcasted_iota(jnp.int32, table.shape, 1), GATE_LANES // 2)
        acts = []
        for j in (0, 1):
            weight = jnp.sum(jnp.where(which == number[j], table, 0.0), axis=1, keepdims=True)
            pr = jnp.dot(rows_a[:, GATE_LANES:], gu[j, 0:cut, :], preferred_element_type=f32)
            pr = pr + jnp.dot(rows_b, gu[j, cut:cut + b, :], preferred_element_type=f32)
            g, u = pr[:, 0:128], pr[:, 128:256]
            acts.append((g / (1.0 + jnp.exp(-g)) * u * weight).astype(bf))
        o = jnp.dot(acts[0], dn[0], preferred_element_type=f32) + jnp.dot(acts[1], dn[1], preferred_element_type=f32)
        for i, zz in enumerate(zs):
            block = o[i * NY * n:(i + 1) * NY * n]
            pa[zz] = block[:, 0:f].reshape(NY, n, f)
            pb[zz] = block[:, f:2 * f].reshape(NY, n, f)
            by_s[zz] = block[:, f:2 * f].astype(bf).reshape(NY, n, f)
            for k in AWAY:
                send(by_s.at[zz, yc(k)], by_r.at[zz, y], rby_s.at[zz, k], rby_r.at[zz, y], at(yc(k), z))

    def chunk(s):
        zs = [zc(s)] if s in (0, opp) else [zc(-s), zc(s)]
        for zz in zs:
            for k in AWAY:
                took(gb.at[zz, yc(k)], b2_s.at[0, k], b2_r.at[zz, yc(k)], at(yc(k), z))
        compute(zs)

    def a_send(d, k, i, value):
        sa[d, k, i] = value.astype(bf)
        send(sa.at[d, k, i], ra.at[d, k, i], rsa_s.at[d, k, i], rsa_r.at[d, k, i], nbr[d])

    def a_took(d, k, i):
        took(ra.at[d, k, i], rsa_s.at[d, k, i], rsa_r.at[d, k, i], nbr[d])
        return ra[d, k, i].astype(f32)

    h = b // 2
    for s in range(1, opp + 1):
        for d in (0, 1):
            zz = zc(-s) if d == 0 else zc(s)
            if s < opp:
                took(gb.at[zz, y], b1_s.at[d, s], b1_r.at[d, s], nbr[d])
                block = gb.at[zz, y] if s + 1 < opp else gb.at[zz, y, :, d * h:(d + 1) * h]
                send(block, block, b1_s.at[d, s + 1], b1_r.at[d, s + 1], nbr[d])
            else:
                block = gb.at[zz, y, :, d * h:(d + 1) * h]
                took(block, b1_s.at[d, s], b1_r.at[d, s], nbr[d])
            if s < opp or d == 1:
                for k in AWAY:
                    send(gb.at[zz, y], gb.at[zz, y], b2_s.at[2 * s - 1 + d if s < opp else 2 * s - 1, k], b2_r.at[zz, y], at(yc(k), z))
        if s == opp:
            chunk(2)
            chunk(3)
            for d in (0, 1):
                for i in REL[1 - d]:
                    a_send(d, opp - 1, i, pa[zc(opp - 1) if d == 0 else zc(1 - opp), yc(i)])
        for i in ORDER:
            for d in (0, 1):
                if s == opp and i not in REL[d]:
                    continue
                zz = zc(-s) if d == 0 else zc(s)
                yb = yc(i)
                took(ga.at[zz, yb], a2_s.at[d, s, i], a2_r.at[d, s, i], nbr[d])
                if s + 1 < opp or (s + 1 == opp and i in REL[d]):
                    send(ga.at[zz, yb], ga.at[zz, yb], a2_s.at[d, s + 1, i], a2_r.at[d, s + 1, i], nbr[d])
        if s in (2, 3):
            chunk(s - 2)
    chunk(opp)

    def a_step(k):
        for i in ORDER:
            for d in (0, 1):
                if k >= opp - 1 and i not in REL[d]:
                    continue
                value = pa[zc(k) if d == 0 else zc(-k), yc(i)]
                if k < opp:
                    value = value + a_took(d, k + 1, i)
                a_send(d, k, i, value)

    def b_own(zz):
        value = pb[zz, y]
        for k in AWAY:
            took(by_r.at[zz, yc(k)], rby_s.at[zz, k], rby_r.at[zz, yc(k)], at(yc(k), z))
            value = value + by_r[zz, yc(k)].astype(f32)
        return value

    e = f // 2

    def b_step(k):
        if k == opp:
            value = b_own(zc(k)).astype(bf)
            for d in (0, 1):
                lanes = slice(d * e, (d + 1) * e)
                sb[d, k, :, lanes] = value[:, lanes]
                send(sb.at[d, k, :, lanes], rb.at[d, k, :, lanes], rsb_s.at[d, k], rsb_r.at[d, k], nbr[d])
            return
        for d in (0, 1):
            value = b_own(zc(k) if d == 0 else zc(-k))
            if k == opp - 1:
                lanes = slice(d * e, (d + 1) * e)
                took(rb.at[d, k + 1, :, lanes], rsb_s.at[d, k + 1], rsb_r.at[d, k + 1], nbr[d])
                added = value[:, lanes] + rb[d, k + 1, :, lanes].astype(f32)
                value = jnp.concatenate([added, value[:, e:]] if d == 0 else [value[:, :e], added], axis=1)
            else:
                took(rb.at[d, k + 1], rsb_s.at[d, k + 1], rsb_r.at[d, k + 1], nbr[d])
                value = value + rb[d, k + 1].astype(f32)
            sb[d, k] = value.astype(bf)
            send(sb.at[d, k], rb.at[d, k], rsb_s.at[d, k], rsb_r.at[d, k], nbr[d])

    a_step(4)
    a_step(3)
    b_step(4)
    a_step(2)
    b_step(3)
    a_step(1)
    b_step(2)
    for k in AWAY:
        yb = yc(k)
        ys[yb] = (pa[z, yb] + a_took(0, 1, k) + a_took(1, 1, k)).astype(bf)
        send(ys.at[yb], yr.at[y], ry_s.at[k], ry_r.at[y], at(yb, z))
    total_a = pa[z, y] + a_took(0, 1, 0) + a_took(1, 1, 0)
    b_step(1)
    total_b = b_own(z)
    for d in (0, 1):
        took(rb.at[d, 1], rsb_s.at[d, 1], rsb_r.at[d, 1], nbr[d])
        total_b = total_b + rb[d, 1].astype(f32)
    for k in AWAY:
        yb = yc(k)
        took(yr.at[yb], ry_s.at[k], ry_r.at[yb], at(yb, z))
        total_a = total_a + yr[yb].astype(f32)

    total = jnp.concatenate([total_a, total_b], axis=1)
    for t in range(n_tp):
        quarter = total[:, t * width:(t + 1) * width]
        xf[t] = quarter
        xs[t] = quarter.astype(bf)
    for k in AWAY:
        t = tc(k)
        send(xs.at[t], xr.at[tp], rx_s.at[k], rx_r.at[tp], {"tp": t})
    value = xf[n_tp] + xf[tp]
    for k in AWAY:
        t = tc(k)
        took(xr.at[t], rx_s.at[k], rx_r.at[t], {"tp": t})
        value = value + xr[t].astype(f32)
    out[...] = value.astype(bf)
    for c in pending:
        c.wait_send()


def layer(
    hidden, lengths, migrate, kv_cache, attn_gain, moe_gain, w_query, key_value_weight, output_weight,
    w_gateup, w_down, expert_ids, expert_gates,
):
    n_tp, n_req = lax.axis_size("tp"), lax.axis_size("req")
    n, width = hidden.shape
    model = w_query.shape[0]
    kvh = kv_cache.shape[2]
    kv = kv_cache.reshape(n, kv_cache.shape[1] * kvh, kv_cache.shape[3])
    lanes = kv.shape[1]
    i = np.arange(128) % (HEAD_SIZE // 2)
    freq = jnp.asarray((ROPE_BASE ** (-2.0 * i / HEAD_SIZE)).astype(np.float32)[None])
    ag, mg = attn_gain.reshape(-1, 128), moe_gain.reshape(-1, 128)
    ids, gates = expert_ids.T, expert_gates.T
    f = b = model // 2
    a = GATE_LANES + model - b
    gu = w_gateup.reshape(2 * model, w_gateup.shape[3])
    dn = w_down[0]
    bf, f32 = jnp.bfloat16, jnp.float32
    dma, v = pltpu.SemaphoreType.DMA, pltpu.VMEM
    k5 = NZ // 2 + 1
    args = (lengths, migrate, hidden, kv, ag, mg, freq, w_query, key_value_weight, output_weight, ids, gates, gu, dn)
    return pl.pallas_call(
        functools.partial(layer_kernel, n_tp, n_req),
        name="layer",
        out_shape=jax.ShapeDtypeStruct((n, width), bf),
        in_specs=[pl.BlockSpec(memory_space=pltpu.SMEM if i == 1 else pltpu.HBM) for i in range(len(args))],
        out_specs=pl.BlockSpec(memory_space=pltpu.VMEM),
        scratch_shapes=[
            pltpu.SMEM(lengths.shape, jnp.int32),
            v(hidden.shape, bf), v(ag.shape, f32), v(mg.shape, f32), v(freq.shape, f32), v(ids.shape, jnp.int32), v(gates.shape, f32),
            v(kv.shape, bf), v(w_query.shape, bf), v(key_value_weight.shape, bf), v(output_weight.shape, bf),
            v((2, n_tp, n, width), bf), v(kv.shape[1:], bf), v(kv.shape[1:], bf), v((n, model), bf), v((n_tp, n, model), bf),
            v((n, 8, 128), f32), v((n, 8, 128), f32), v((n, 8, 128), f32), v((8, lanes), f32),
            v((NZ, NY, n, a), bf), v((NZ, NY, n, b), bf), v((NZ, NY, n, f), f32), v((NZ, NY, n, f), f32),
            v((2,) + gu.shape, bf), v((512, 128), f32), v((2, model, 256), bf), v((2,) + dn.shape, bf),
            v((NZ, NY, n, f), bf), v((NZ, NY, n, f), bf),
            v((2, k5, NY, n, f), bf), v((2, k5, NY, n, f), bf), v((2, k5, n, f), bf), v((2, k5, n, f), bf),
            v((NY, n, f), bf), v((NY, n, f), bf), v((n_tp, n, width), bf), v((n_tp, n, width), bf), v((n_tp + 1, n, width), f32),
            dma((16,)), dma((n,)), dma((2 * n_tp,)), dma((2, n_tp)), dma, dma, dma((n_tp,)), dma((n_tp,)),
            dma((2,)), dma((2,)), dma((NY,)), dma((NY,)), dma((2, k5, NY)), dma((2, k5, NY)), dma((2, k5)), dma((2, k5)),
            dma((NZ, NY)), dma((NZ, NY)),
            dma((NZ, NY)), dma((NZ, NY)), dma((2, k5, NY)), dma((2, k5, NY)), dma((2, k5)), dma((2, k5)), dma((NY,)), dma((NY,)),
            dma((n_tp,)), dma((n_tp,)),
        ],
        compiler_params=pltpu.CompilerParams(collective_id=0, has_side_effects=True, vmem_limit_bytes=VMEM_LIMIT),
        cost_estimate=pl.CostEstimate(flops=1_500_000_000, bytes_accessed=16_000_000, transcendentals=1_000_000),
    )(*args)


def solution(mesh):
    placed = (
        P(("rep", "req"), "tp"),
        P(None, "req"),
        P("req"),
        P(("rep", "req"), None, "tp", None),
        P(),
        P(),
        P(None, "tp"),
        P(None, "tp"),
        P("tp", None),
        P(("rep", "req"), None, None, "tp"),
        P(("rep", "req"), "tp", None),
        P(("rep", "req"), None),
        P(("rep", "req"), None),
    )
    return jax.shard_map(
        layer, mesh=mesh, in_specs=placed, out_specs=P(("rep", "req"), "tp"), check_vma=False
    )
```

```python
import functools
import jax
import jax.numpy as jnp
import numpy as np
from jax import lax
from jax.experimental import pallas as pl
from jax.experimental.pallas import tpu as pltpu
from jax.sharding import PartitionSpec as P

MESH = pl.DeviceIdType.MESH
HEAD_SIZE = 64
EPSILON = 1e-06
ROPE_BASE = 10000.0
MASKED = -1e30
GATE_LANES = 128
NY, NZ = 4, 8
VMEM_LIMIT = 58 * 2**20
A_LANES, FA_LANES = 896, 768


def rows_of(scalars, n):
    row = lax.broadcasted_iota(jnp.int32, (n, 128), 0)
    out = jnp.zeros((n, 128), jnp.int32)
    for r in range(n):
        out = jnp.where(row == r, scalars(r), out)
    return out


def attend(q, kvn, kv, bias, limit):
    scale = HEAD_SIZE ** (-0.5)
    s = lax.dot_general(q.astype(jnp.bfloat16), kv, (((1,), (1,)), ((), ())), preferred_element_type=jnp.float32)
    lane = lax.broadcasted_iota(jnp.int32, s.shape, 1)
    s = jnp.where(lane < limit, s * scale + bias, MASKED)
    own = jnp.sum(q * kvn, axis=1, keepdims=True) * scale
    peak = jnp.maximum(jnp.max(s, axis=1, keepdims=True), own)
    p = jnp.exp(s - peak)
    p_own = jnp.exp(own - peak)
    inv = 1.0 / (jnp.sum(p, axis=1, keepdims=True) + p_own)
    w = (p * inv).astype(jnp.bfloat16)
    w_own = (p_own * inv).astype(jnp.bfloat16).astype(jnp.float32)
    return jnp.dot(w, kv, preferred_element_type=jnp.float32) + w_own * kvn


def layer_kernel(
    n_tp, n_req,
    len_h, mig_s, hid_h, kv_h, ag_h, mg_h, freq_h, wq_h, wkv_h, wo_h, ids_h, gates_h, gu_h, dn_h,
    out,
    len_s, hid, ag, mg, freq, ids, gates,
    kv_v, wq_v, wkv_v, wo_v, tok, kv_send, kv_recv, part_send, part_recv, q_s, kvn_s, ctx_s, bias_s,
    ga, gb, pa, pb, raw, wide, gu, dn,
    by_s, by_r, sa, ra, sb, rb, ys, yr, xs, xr, xf,
    load_sem, kv_sem, tok_send_sem, tok_recv_sem, kv_send_sem, kv_recv_sem, part_send_sem, part_recv_sem,
    wx_s, wx_r, a1_s, a1_r, a2_s, a2_r, b1_s, b1_r, b2_s, b2_r,
    rby_s, rby_r, rsa_s, rsa_r, rsb_s, rsb_r, ry_s, ry_r, rx_s, rx_r,
):
    rep, req, tp = lax.axis_index("rep"), lax.axis_index("req"), lax.axis_index("tp")
    y, z = req // NZ, lax.rem(req, NZ)
    n, width = hid.shape
    heads = wq_v.shape[1] // HEAD_SIZE
    kvh = wkv_v.shape[1] // (2 * HEAD_SIZE)
    group = heads // kvh
    n_lanes = kv_v.shape[1]
    a, b, fa, fb = ga.shape[-1], gb.shape[-1], pa.shape[-1], pb.shape[-1]
    opp = NZ // 2
    part_b = (slice(0, b // 256 * 128), slice(b // 256 * 128, b))
    part_fb = (slice(0, fb // 256 * 128), slice(fb // 256 * 128, fb))
    bf, f32 = jnp.bfloat16, jnp.float32

    def zc(k):
        return lax.rem(z + (k + NZ), NZ)

    def yc(k):
        return lax.rem(y + k, NY)

    def tc(k):
        return lax.rem(tp + k, n_tp)

    def at(yy, zz):
        return {"req": yy * NZ + zz}

    nbr = (at(y, zc(1)), at(y, zc(-1)))
    partner = {"rep": 1 - rep}
    pending = []

    def rcopy(src, dst, ssem, rsem, dev):
        return pltpu.make_async_remote_copy(src_ref=src, dst_ref=dst, send_sem=ssem, recv_sem=rsem, device_id=dev, device_id_type=MESH)

    def send(*args):
        c = rcopy(*args)
        c.start()
        pending.append(c)

    def took(dst, ssem, rsem, dev):
        rcopy(dst, dst, ssem, rsem, dev).wait_recv()

    loads = []

    def load(src, dst):
        c = pltpu.make_async_copy(src, dst, load_sem.at[len(loads)])
        c.start()
        loads.append(c)
        return c

    small = [load(*p) for p in ((hid_h, hid), (len_h, len_s), (ids_h, ids), (gates_h, gates), (freq_h, freq), (ag_h, ag), (mg_h, mg))]
    proj = [load(wq_h, wq_v), load(wkv_h, wkv_v)]
    kv_loads = [pltpu.make_async_copy(kv_h.at[r], kv_v.at[r], kv_sem.at[r]) for r in range(n)]
    for c in kv_loads:
        c.start()
    load_o = load(wo_h, wo_v)
    own_gu = load(gu_h, raw.at[0])
    own_dn = load(dn_h, dn.at[0])

    barrier = pltpu.get_barrier_semaphore()
    peers = [(0, tc(k)) for k in range(1, n_tp)] + [(1, tc(k)) for k in range(n_tp)]
    far_rep = lambda side: rep if side == 0 else 1 - rep
    greet = [{"rep": far_rep(side), "tp": t} for side, t in peers]
    greet += [at(yc(k), z) for k in range(1, NY)] + [nbr[0], nbr[1]]
    for dev in greet:
        pl.semaphore_signal(barrier, inc=1, device_id=dev, device_id_type=MESH)
    pl.semaphore_wait(barrier, len(greet))

    for c in small:
        c.wait()
    for i, (side, t) in enumerate(peers):
        send(hid, tok.at[side, tp], tok_send_sem.at[i], tok_recv_sem.at[side, tp], {"rep": far_rep(side), "tp": t})
    tok[0, tp] = hid[...]
    send(gu_h, raw.at[1], wx_s.at[0], wx_r.at[0], partner)
    send(dn_h, dn.at[1], wx_s.at[1], wx_r.at[1], partner)

    slot = mig_s[0]
    row = lax.broadcasted_iota(jnp.int32, (n, 128), 0)
    lane = lax.broadcasted_iota(jnp.int32, (n, 128), 1)
    moved = row == slot
    own_span = rows_of(lambda r: jnp.where(rep == 0, len_s[0, r], len_s[1, r]), n)
    other_span = rows_of(lambda r: jnp.where(rep == 0, len_s[1, r], len_s[0, r]), n)
    span = jnp.where(moved, other_span, own_span).astype(f32)
    angle = span * freq[...]
    cosine, sine = jnp.cos(angle), jnp.sin(angle)
    first = lax.rem(lane, HEAD_SIZE) < HEAD_SIZE // 2
    half = HEAD_SIZE // 2

    def rotate(v):
        turned = jnp.where(first, -pltpu.roll(v, 128 - half, 1), pltpu.roll(v, half, 1))
        return v * cosine + turned * sine

    head = lax.broadcasted_iota(jnp.int32, (8, n_lanes), 0)
    pos = lax.broadcasted_iota(jnp.int32, (8, n_lanes), 1)
    bias_s[...] = jnp.where(lax.rem(pos, kvh) == head // group, 0.0, MASKED)

    eye = lax.broadcasted_iota(jnp.int32, (n, n), 0) == lax.broadcasted_iota(jnp.int32, (n, n), 1)
    expert = lax.rem(lane, GATE_LANES // 2)
    dense = jnp.zeros((n, 128), f32)
    for k in range(ids.shape[0]):
        idc = jnp.sum(jnp.where(eye, ids[k:k + 1, :], 0), axis=1, keepdims=True)
        gc = jnp.sum(jnp.where(eye, gates[k:k + 1, :], 0.0), axis=1, keepdims=True)
        dense = dense + jnp.where(expert == idc, gc, 0.0)
    high = dense.astype(bf).astype(f32)
    ga[z, y, :, 0:GATE_LANES] = jnp.where(lane < GATE_LANES // 2, high, dense - high).astype(bf)

    part = wide.shape[0]

    def split(j):
        def step(i, carry):
            start = pl.multiple_of(i * part, part)
            wide[...] = raw[j, pl.ds(start, part), :].astype(f32)
            rows = pl.ds(pl.multiple_of(i * (part // 2), part // 2), part // 2)
            gu[j, rows, 0:128] = wide[pl.ds(0, part // 2, stride=2), :].astype(bf)
            gu[j, rows, 128:256] = wide[pl.ds(1, part // 2, stride=2), :].astype(bf)
            return carry
        lax.fori_loop(0, raw.shape[1] // part, step, 0)

    for side, t in peers:
        took(tok.at[side, t], tok_send_sem.at[0], tok_recv_sem.at[side, t], {"tp": t})

    moved_w = lax.broadcasted_iota(jnp.int32, (n, width), 0) == slot
    tokens = jnp.concatenate(
        [jnp.where(moved_w, tok[1, t].astype(f32), tok[0, t].astype(f32)) for t in range(n_tp)], axis=1)
    mean = jnp.mean(tokens * tokens, axis=1, keepdims=True)
    gain = jnp.concatenate([ag[i:i + 1, :] for i in range(ag.shape[0])], axis=1)
    normed = (tokens * lax.rsqrt(mean + EPSILON) * gain).astype(bf)
    for c in proj:
        c.wait()
    queries = jnp.dot(normed, wq_v[...], preferred_element_type=f32)
    keyval = jnp.dot(normed, wkv_v[...], preferred_element_type=f32)
    q_s[...] = jnp.zeros_like(q_s)
    kvn_s[...] = jnp.zeros_like(kvn_s)
    low_lanes = lane < HEAD_SIZE
    for i in range(heads // 2):
        turned = rotate(queries[:, i * 128:(i + 1) * 128]).astype(bf).astype(f32)
        q_s[:, 2 * i, :] = jnp.where(low_lanes, turned, 0.0)
        q_s[:, 2 * i + 1, :] = jnp.where(low_lanes, pltpu.roll(turned, HEAD_SIZE, 1), 0.0)
    for g in range(kvh):
        both = keyval[:, g * 128:(g + 1) * 128]
        both = jnp.where(low_lanes, rotate(both), both).astype(bf).astype(f32)
        for h in range(g * group, (g + 1) * group):
            kvn_s[:, h, :] = both

    for c in kv_loads:
        c.wait()
    kv_send[...] = kv_v[slot]
    kv_copy = rcopy(kv_send, kv_recv, kv_send_sem, kv_recv_sem, partner)
    kv_copy.start()

    def one(r):
        limit = kvh * jnp.where(rep == 0, len_s[0, r], len_s[1, r])
        ctx_s[r] = attend(q_s[r], kvn_s[r], kv_v[r], bias_s[...], limit)

    UNROLL = 4

    def step(i, carry):
        for j in range(UNROLL):
            one(i * UNROLL + j)
        return carry

    lax.fori_loop(0, n // UNROLL, step, 0)
    kv_copy.wait()
    limit = kvh * jnp.where(rep == 0, len_s[1, slot], len_s[0, slot])
    arrived = attend(q_s[slot], kvn_s[slot], kv_recv[...], bias_s[...], limit)

    blocks = []
    for i in range(heads // 2):
        even = jnp.where(moved, arrived[2 * i:2 * i + 1], ctx_s[:, 2 * i, :])
        odd = jnp.where(moved, arrived[2 * i + 1:2 * i + 2], ctx_s[:, 2 * i + 1, :])
        blocks.append(jnp.where(low_lanes, pltpu.roll(even, HEAD_SIZE, 1), odd))
    context = jnp.concatenate(blocks, axis=1).astype(bf)
    load_o.wait()
    partial = jnp.dot(context, wo_v[...], preferred_element_type=f32)
    part_send[...] = partial.astype(bf)
    for k in (1, 3, 2):
        send(part_send, part_recv.at[tp], part_send_sem.at[k], part_recv_sem.at[tp], {"tp": tc(k)})
    own_gu.wait()
    own_dn.wait()
    split(0)
    took(raw.at[1], wx_s.at[0], wx_r.at[0], partner)
    took(dn.at[1], wx_s.at[1], wx_r.at[1], partner)
    split(1)
    total = tokens + partial
    for k in (1, 3, 2):
        t = tc(k)
        took(part_recv.at[t], part_send_sem.at[k], part_recv_sem.at[t], {"tp": t})
        total = total + part_recv[t].astype(f32)
    mean = jnp.mean(total * total, axis=1, keepdims=True)
    gain = jnp.concatenate([mg[i:i + 1, :] for i in range(mg.shape[0])], axis=1)
    x = (total * lax.rsqrt(mean + EPSILON) * gain).astype(bf)
    cut = a - GATE_LANES
    ga[z, y, :, GATE_LANES:] = x[:, 0:cut]
    gb[z, y] = x[:, cut:]

    ORDER = (0, 1, 3, 2)
    REL = ((0, 1), (3, 2))
    AWAY = (1, 3, 2)
    for d in (0, 1):
        send(gb.at[z, y], gb.at[z, y], b1_s.at[d, 1], b1_r.at[d, 1], nbr[d])
    for k in AWAY:
        send(ga.at[z, y], ga.at[z, y], a1_s.at[k], a1_r.at[y], at(yc(k), z))
    for d in (0, 1):
        send(ga.at[z, y], ga.at[z, y], a2_s.at[d, 1, 0], a2_r.at[d, 1, 0], nbr[d])
    for k in AWAY:
        send(gb.at[z, y], gb.at[z, y], b2_s.at[0, k], b2_r.at[z, y], at(yc(k), z))
    own = jnp.zeros((n, width), f32)
    for t in range(n_tp):
        own = jnp.where(tp == t, total[:, t * width:(t + 1) * width], own)
    xf[n_tp] = own
    number = (rep * n_req + req, (1 - rep) * n_req + req)

    def compute(zs):
        rows_a = jnp.concatenate([ga[zz].reshape(NY * n, a) for zz in zs], axis=0)
        rows_b = jnp.concatenate([gb[zz].reshape(NY * n, b) for zz in zs], axis=0)
        table = rows_a[:, 0:GATE_LANES].astype(f32)
        which = lax.rem(lax.broadcasted_iota(jnp.int32, table.shape, 1), GATE_LANES // 2)
        acts = []
        for j in (0, 1):
            weight = jnp.sum(jnp.where(which == number[j], table, 0.0), axis=1, keepdims=True)
            pr = jnp.dot(rows_a[:, GATE_LANES:], gu[j, 0:cut, :], preferred_element_type=f32)
            pr = pr + jnp.dot(rows_b, gu[j, cut:cut + b, :], preferred_element_type=f32)
            g, u = pr[:, 0:128], pr[:, 128:256]
            acts.append((g / (1.0 + jnp.exp(-g)) * u * weight).astype(bf))
        o = jnp.dot(acts[0], dn[0], preferred_element_type=f32) + jnp.dot(acts[1], dn[1], preferred_element_type=f32)
        for i, zz in enumerate(zs):
            block = o[i * NY * n:(i + 1) * NY * n]
            pa[zz] = block[:, 0:fa].reshape(NY, n, fa)
            pb[zz] = block[:, fa:].reshape(NY, n, fb)
            by_s[zz] = block[:, fa:].astype(bf).reshape(NY, n, fb)
            for k in AWAY:
                send(by_s.at[zz, yc(k)], by_r.at[zz, y], rby_s.at[zz, k], rby_r.at[zz, y], at(yc(k), z))

    def chunks(*steps):
        zs = []
        for s in steps:
            zs += [zc(s)] if s in (0, opp) else [zc(-s), zc(s)]
        for zz in zs:
            for k in AWAY:
                took(gb.at[zz, yc(k)], b2_s.at[0, k], b2_r.at[zz, yc(k)], at(yc(k), z))
        compute(zs)

    def a_send(d, k, i, value):
        sa[d, k, i] = value.astype(bf)
        send(sa.at[d, k, i], ra.at[d, k, i], rsa_s.at[d, k, i], rsa_r.at[d, k, i], nbr[d])

    def a_took(d, k, i):
        took(ra.at[d, k, i], rsa_s.at[d, k, i], rsa_r.at[d, k, i], nbr[d])
        return ra[d, k, i].astype(f32)

    def pass_b(s):
        for d in (0, 1):
            zz = zc(-s) if d == 0 else zc(s)
            if s < opp:
                took(gb.at[zz, y], b1_s.at[d, s], b1_r.at[d, s], nbr[d])
                block = gb.at[zz, y] if s + 1 < opp else gb.at[zz, y, :, part_b[d]]
                send(block, block, b1_s.at[d, s + 1], b1_r.at[d, s + 1], nbr[d])
            else:
                took(gb.at[zz, y, :, part_b[d]], b1_s.at[d, s], b1_r.at[d, s], nbr[d])
        for d in (0, 1) if s < opp else (0,):
            zz = zc(-s) if d == 0 else zc(s)
            for k in AWAY:
                send(gb.at[zz, y], gb.at[zz, y], b2_s.at[2 * s - 1 + d, k], b2_r.at[zz, y], at(yc(k), z))

    def pass_a(s):
        for i in ORDER:
            for d in (0, 1):
                if s == opp and i not in REL[d]:
                    continue
                zz = zc(-s) if d == 0 else zc(s)
                yb = yc(i)
                if s:
                    took(ga.at[zz, yb], a2_s.at[d, s, i], a2_r.at[d, s, i], nbr[d])
                elif i == 0:
                    continue
                elif d == 0:
                    took(ga.at[z, yb], a1_s.at[i], a1_r.at[yb], at(yb, z))
                if s + 1 < opp or (s + 1 == opp and i in REL[d]):
                    send(ga.at[zz, yb], ga.at[zz, yb], a2_s.at[d, s + 1, i], a2_r.at[d, s + 1, i], nbr[d])

    pass_b(1)
    pass_a(0)
    pass_b(2)
    pass_a(1)
    pass_b(3)
    pass_a(2)
    pass_b(4)
    chunks(0, 1)
    pass_a(3)
    chunks(2, 3)
    for d in (0, 1):
        for i in REL[1 - d]:
            a_send(d, opp - 1, i, pa[zc(opp - 1) if d == 0 else zc(1 - opp), yc(i)])
    pass_a(4)
    chunks(4)

    def a_step(k):
        for i in ORDER:
            for d in (0, 1):
                if k >= opp - 1 and i not in REL[d]:
                    continue
                value = pa[zc(k) if d == 0 else zc(-k), yc(i)]
                if k < opp:
                    value = value + a_took(d, k + 1, i)
                a_send(d, k, i, value)

    def b_own(zz):
        value = pb[zz, y]
        for k in AWAY:
            took(by_r.at[zz, yc(k)], rby_s.at[zz, k], rby_r.at[zz, yc(k)], at(yc(k), z))
            value = value + by_r[zz, yc(k)].astype(f32)
        return value

    def b_step(k):
        if k == opp:
            value = b_own(zc(k)).astype(bf)
            for d in (0, 1):
                lanes = part_fb[d]
                sb[d, k, :, lanes] = value[:, lanes]
                send(sb.at[d, k, :, lanes], rb.at[d, k, :, lanes], rsb_s.at[d, k], rsb_r.at[d, k], nbr[d])
            return
        for d in (0, 1):
            value = b_own(zc(k) if d == 0 else zc(-k))
            if k == opp - 1:
                lanes = part_fb[d]
                took(rb.at[d, k + 1, :, lanes], rsb_s.at[d, k + 1], rsb_r.at[d, k + 1], nbr[d])
                added = value[:, lanes] + rb[d, k + 1, :, lanes].astype(f32)
                value = jnp.concatenate([added, value[:, part_fb[1]]] if d == 0 else [value[:, part_fb[0]], added], axis=1)
            else:
                took(rb.at[d, k + 1], rsb_s.at[d, k + 1], rsb_r.at[d, k + 1], nbr[d])
                value = value + rb[d, k + 1].astype(f32)
            sb[d, k] = value.astype(bf)
            send(sb.at[d, k], rb.at[d, k], rsb_s.at[d, k], rsb_r.at[d, k], nbr[d])

    a_step(4)
    a_step(3)
    b_step(4)
    a_step(2)
    b_step(3)
    a_step(1)
    b_step(2)
    for k in AWAY:
        yb = yc(k)
        ys[yb] = (pa[z, yb] + a_took(0, 1, k) + a_took(1, 1, k)).astype(bf)
        send(ys.at[yb], yr.at[y], ry_s.at[k], ry_r.at[y], at(yb, z))
    total_a = pa[z, y] + a_took(0, 1, 0) + a_took(1, 1, 0)
    b_step(1)
    total_b = b_own(z)
    for d in (0, 1):
        took(rb.at[d, 1], rsb_s.at[d, 1], rsb_r.at[d, 1], nbr[d])
        total_b = total_b + rb[d, 1].astype(f32)
    for k in AWAY:
        yb = yc(k)
        took(yr.at[yb], ry_s.at[k], ry_r.at[yb], at(yb, z))
        total_a = total_a + yr[yb].astype(f32)

    total = jnp.concatenate([total_a, total_b], axis=1)
    for t in range(n_tp):
        quarter = total[:, t * width:(t + 1) * width]
        xf[t] = quarter
        xs[t] = quarter.astype(bf)
    for k in AWAY:
        t = tc(k)
        send(xs.at[t], xr.at[tp], rx_s.at[k], rx_r.at[tp], {"tp": t})
    value = xf[n_tp] + xf[tp]
    for k in AWAY:
        t = tc(k)
        took(xr.at[t], rx_s.at[k], rx_r.at[t], {"tp": t})
        value = value + xr[t].astype(f32)
    out[...] = value.astype(bf)
    for c in pending:
        c.wait_send()


def layer(
    hidden, lengths, migrate, kv_cache, attn_gain, moe_gain, w_query, key_value_weight, output_weight,
    w_gateup, w_down, expert_ids, expert_gates,
):
    n_tp, n_req = lax.axis_size("tp"), lax.axis_size("req")
    n, width = hidden.shape
    model = w_query.shape[0]
    kvh = kv_cache.shape[2]
    kv = kv_cache.reshape(n, kv_cache.shape[1] * kvh, kv_cache.shape[3])
    lanes = kv.shape[1]
    i = np.arange(128) % (HEAD_SIZE // 2)
    freq = jnp.asarray((ROPE_BASE ** (-2.0 * i / HEAD_SIZE)).astype(np.float32)[None])
    ag, mg = attn_gain.reshape(-1, 128), moe_gain.reshape(-1, 128)
    ids, gates = expert_ids.T, expert_gates.T
    a, fa = A_LANES, FA_LANES
    b, fb = GATE_LANES + model - a, model - fa
    gu = w_gateup.reshape(2 * model, w_gateup.shape[3])
    dn = w_down[0]
    bf, f32 = jnp.bfloat16, jnp.float32
    dma, v = pltpu.SemaphoreType.DMA, pltpu.VMEM
    k5 = NZ // 2 + 1
    args = (lengths, migrate, hidden, kv, ag, mg, freq, w_query, key_value_weight, output_weight, ids, gates, gu, dn)
    return pl.pallas_call(
        functools.partial(layer_kernel, n_tp, n_req),
        name="layer",
        out_shape=jax.ShapeDtypeStruct((n, width), bf),
        in_specs=[pl.BlockSpec(memory_space=pltpu.SMEM if i == 1 else pltpu.HBM) for i in range(len(args))],
        out_specs=pl.BlockSpec(memory_space=pltpu.VMEM),
        scratch_shapes=[
            pltpu.SMEM(lengths.shape, jnp.int32),
            v(hidden.shape, bf), v(ag.shape, f32), v(mg.shape, f32), v(freq.shape, f32), v(ids.shape, jnp.int32), v(gates.shape, f32),
            v(kv.shape, bf), v(w_query.shape, bf), v(key_value_weight.shape, bf), v(output_weight.shape, bf),
            v((2, n_tp, n, width), bf), v(kv.shape[1:], bf), v(kv.shape[1:], bf), v((n, model), bf), v((n_tp, n, model), bf),
            v((n, 8, 128), f32), v((n, 8, 128), f32), v((n, 8, 128), f32), v((8, lanes), f32),
            v((NZ, NY, n, a), bf), v((NZ, NY, n, b), bf), v((NZ, NY, n, fa), f32), v((NZ, NY, n, fb), f32),
            v((2,) + gu.shape, bf), v((512, 128), f32), v((2, model, 256), bf), v((2,) + dn.shape, bf),
            v((NZ, NY, n, fb), bf), v((NZ, NY, n, fb), bf),
            v((2, k5, NY, n, fa), bf), v((2, k5, NY, n, fa), bf), v((2, k5, n, fb), bf), v((2, k5, n, fb), bf),
            v((NY, n, fa), bf), v((NY, n, fa), bf), v((n_tp, n, width), bf), v((n_tp, n, width), bf), v((n_tp + 1, n, width), f32),
            dma((16,)), dma((n,)), dma((2 * n_tp,)), dma((2, n_tp)), dma, dma, dma((n_tp,)), dma((n_tp,)),
            dma((2,)), dma((2,)), dma((NY,)), dma((NY,)), dma((2, k5, NY)), dma((2, k5, NY)), dma((2, k5)), dma((2, k5)),
            dma((NZ, NY)), dma((NZ, NY)),
            dma((NZ, NY)), dma((NZ, NY)), dma((2, k5, NY)), dma((2, k5, NY)), dma((2, k5)), dma((2, k5)), dma((NY,)), dma((NY,)),
            dma((n_tp,)), dma((n_tp,)),
        ],
        compiler_params=pltpu.CompilerParams(collective_id=0, has_side_effects=True, vmem_limit_bytes=VMEM_LIMIT),
        cost_estimate=pl.CostEstimate(flops=1_500_000_000, bytes_accessed=16_000_000, transcendentals=1_000_000),
    )(*args)


def solution(mesh):
    placed = (
        P(("rep", "req"), "tp"),
        P(None, "req"),
        P("req"),
        P(("rep", "req"), None, "tp", None),
        P(),
        P(),
        P(None, "tp"),
        P(None, "tp"),
        P("tp", None),
        P(("rep", "req"), None, None, "tp"),
        P(("rep", "req"), "tp", None),
        P(("rep", "req"), None),
        P(("rep", "req"), None),
    )
    return jax.shard_map(
        layer, mesh=mesh, in_specs=placed, out_specs=P(("rep", "req"), "tp"), check_vma=False
    )
```

```python
import functools
import jax
import jax.numpy as jnp
import numpy as np
from jax import lax
from jax.experimental import pallas as pl
from jax.experimental.pallas import tpu as pltpu
from jax.sharding import PartitionSpec as P

MESH = pl.DeviceIdType.MESH
HEAD_SIZE = 64
EPSILON = 1e-06
ROPE_BASE = 10000.0
MASKED = -1e30
GATE_LANES = 128
NY, NZ = 4, 8
VMEM_LIMIT = 58 * 2**20
A_LANES, FA_LANES = 896, 768


def rows_of(scalars, n):
    row = lax.broadcasted_iota(jnp.int32, (n, 128), 0)
    out = jnp.zeros((n, 128), jnp.int32)
    for r in range(n):
        out = jnp.where(row == r, scalars(r), out)
    return out


def attend(requests, bias):
    scale = HEAD_SIZE ** (-0.5)
    scores, owns = [], []
    for q, kvn, kv, limit in requests:
        s = lax.dot_general(q.astype(jnp.bfloat16), kv, (((1,), (1,)), ((), ())), preferred_element_type=jnp.float32)
        place = lax.broadcasted_iota(jnp.int32, s.shape, 1)
        scores.append(jnp.where(place < limit, s * scale + bias, MASKED)[None])
        owns.append((jnp.sum(q * kvn, axis=1, keepdims=True) * scale)[None])
    s, own = jnp.concatenate(scores, axis=0), jnp.concatenate(owns, axis=0)
    peak = jnp.maximum(jnp.max(s, axis=2, keepdims=True), own)
    p = jnp.exp(s - peak)
    p_own = jnp.exp(own - peak)
    inv = 1.0 / (jnp.sum(p, axis=2, keepdims=True) + p_own)
    w = (p * inv).astype(jnp.bfloat16)
    w_own = (p_own * inv).astype(jnp.bfloat16).astype(jnp.float32)
    return [jnp.dot(w[g], kv, preferred_element_type=jnp.float32) + w_own[g] * kvn for g, (q, kvn, kv, limit) in enumerate(requests)]


def layer_kernel(
    n_tp, n_req,
    len_h, mig_s, hid_h, kv_h, ag_h, mg_h, freq_h, wq_h, wkv_h, wo_h, ids_h, gates_h, gu_h, dn_h,
    out,
    len_s, hid, ag, mg, freq, ids, gates,
    kv_v, wq_v, wkv_v, wo_v, tok, kv_send, kv_recv, part_send, part_recv, q_s, kvn_s, ctx_s, bias_s,
    ga, gb, pa, pb, raw, wide, gu, dn,
    by_s, by_r, sa, ra, sb, rb, ys, yr, xs, xr, xf,
    load_sem, kv_sem, tok_send_sem, tok_recv_sem, kv_send_sem, kv_recv_sem, part_send_sem, part_recv_sem,
    wx_s, wx_r, a1_s, a1_r, a2_s, a2_r, b1_s, b1_r, b2_s, b2_r,
    rby_s, rby_r, rsa_s, rsa_r, rsb_s, rsb_r, ry_s, ry_r, rx_s, rx_r,
):
    rep, req, tp = lax.axis_index("rep"), lax.axis_index("req"), lax.axis_index("tp")
    y, z = req // NZ, lax.rem(req, NZ)
    n, width = hid.shape
    heads = wq_v.shape[1] // HEAD_SIZE
    kvh = wkv_v.shape[1] // (2 * HEAD_SIZE)
    group = heads // kvh
    n_lanes = kv_v.shape[1]
    a, b, fa, fb = ga.shape[-1], gb.shape[-1], pa.shape[-1], pb.shape[-1]
    opp = NZ // 2
    part_b = (slice(0, b // 256 * 128), slice(b // 256 * 128, b))
    part_fb = (slice(0, fb // 256 * 128), slice(fb // 256 * 128, fb))
    bf, f32 = jnp.bfloat16, jnp.float32

    def zc(k):
        return lax.rem(z + (k + NZ), NZ)

    def yc(k):
        return lax.rem(y + k, NY)

    def tc(k):
        return lax.rem(tp + k, n_tp)

    def at(yy, zz):
        return {"req": yy * NZ + zz}

    nbr = (at(y, zc(1)), at(y, zc(-1)))
    partner = {"rep": 1 - rep}
    pending = []

    def rcopy(src, dst, ssem, rsem, dev):
        return pltpu.make_async_remote_copy(src_ref=src, dst_ref=dst, send_sem=ssem, recv_sem=rsem, device_id=dev, device_id_type=MESH)

    def send(*args):
        c = rcopy(*args)
        c.start()
        pending.append(c)

    def took(dst, ssem, rsem, dev):
        rcopy(dst, dst, ssem, rsem, dev).wait_recv()

    loads = []

    def load(src, dst):
        c = pltpu.make_async_copy(src, dst, load_sem.at[len(loads)])
        c.start()
        loads.append(c)
        return c

    small = [load(*p) for p in ((hid_h, hid), (len_h, len_s), (ids_h, ids), (gates_h, gates), (freq_h, freq), (ag_h, ag), (mg_h, mg))]
    proj = [load(wq_h, wq_v), load(wkv_h, wkv_v)]
    kv_loads = [pltpu.make_async_copy(kv_h.at[r], kv_v.at[r], kv_sem.at[r]) for r in range(n)]
    for c in kv_loads:
        c.start()
    load_o = load(wo_h, wo_v)
    own_gu = load(gu_h, raw.at[0])
    own_dn = load(dn_h, dn.at[0])

    barrier = pltpu.get_barrier_semaphore()
    peers = [(0, tc(k)) for k in range(1, n_tp)] + [(1, tc(k)) for k in range(n_tp)]
    far_rep = lambda side: rep if side == 0 else 1 - rep
    greet = [{"rep": far_rep(side), "tp": t} for side, t in peers]
    greet += [at(yc(k), z) for k in range(1, NY)] + [nbr[0], nbr[1]]
    for dev in greet:
        pl.semaphore_signal(barrier, inc=1, device_id=dev, device_id_type=MESH)
    pl.semaphore_wait(barrier, len(greet))

    for c in small:
        c.wait()
    for i, (side, t) in enumerate(peers):
        send(hid, tok.at[side, tp], tok_send_sem.at[i], tok_recv_sem.at[side, tp], {"rep": far_rep(side), "tp": t})
    tok[0, tp] = hid[...]
    send(gu_h, raw.at[1], wx_s.at[0], wx_r.at[0], partner)
    send(dn_h, dn.at[1], wx_s.at[1], wx_r.at[1], partner)

    slot = mig_s[0]
    row = lax.broadcasted_iota(jnp.int32, (n, 128), 0)
    lane = lax.broadcasted_iota(jnp.int32, (n, 128), 1)
    moved = row == slot
    own_span = rows_of(lambda r: jnp.where(rep == 0, len_s[0, r], len_s[1, r]), n)
    other_span = rows_of(lambda r: jnp.where(rep == 0, len_s[1, r], len_s[0, r]), n)
    span = jnp.where(moved, other_span, own_span).astype(f32)
    angle = span * freq[...]
    cosine, sine = jnp.cos(angle), jnp.sin(angle)
    first = lax.rem(lane, HEAD_SIZE) < HEAD_SIZE // 2
    half = HEAD_SIZE // 2

    def rotate(v):
        turned = jnp.where(first, -pltpu.roll(v, 128 - half, 1), pltpu.roll(v, half, 1))
        return v * cosine + turned * sine

    head = lax.broadcasted_iota(jnp.int32, bias_s.shape, 0)
    pos = lax.broadcasted_iota(jnp.int32, bias_s.shape, 1)
    bias_s[...] = jnp.where(lax.rem(pos, kvh) == head // group, 0.0, MASKED)

    eye = lax.broadcasted_iota(jnp.int32, (n, n), 0) == lax.broadcasted_iota(jnp.int32, (n, n), 1)
    expert = lax.rem(lane, GATE_LANES // 2)
    dense = jnp.zeros((n, 128), f32)
    for k in range(ids.shape[0]):
        idc = jnp.sum(jnp.where(eye, ids[k:k + 1, :], 0), axis=1, keepdims=True)
        gc = jnp.sum(jnp.where(eye, gates[k:k + 1, :], 0.0), axis=1, keepdims=True)
        dense = dense + jnp.where(expert == idc, gc, 0.0)
    high = dense.astype(bf).astype(f32)
    ga[z, y, :, 0:GATE_LANES] = jnp.where(lane < GATE_LANES // 2, high, dense - high).astype(bf)

    part = wide.shape[0]

    def split(j):
        def step(i, carry):
            start = pl.multiple_of(i * part, part)
            wide[...] = raw[j, pl.ds(start, part), :].astype(f32)
            rows = pl.ds(pl.multiple_of(i * (part // 2), part // 2), part // 2)
            gu[j, rows, 0:128] = wide[pl.ds(0, part // 2, stride=2), :].astype(bf)
            gu[j, rows, 128:256] = wide[pl.ds(1, part // 2, stride=2), :].astype(bf)
            return carry
        lax.fori_loop(0, raw.shape[1] // part, step, 0)

    for side, t in peers:
        took(tok.at[side, t], tok_send_sem.at[0], tok_recv_sem.at[side, t], {"tp": t})

    moved_w = lax.broadcasted_iota(jnp.int32, (n, width), 0) == slot
    tokens = jnp.concatenate(
        [jnp.where(moved_w, tok[1, t].astype(f32), tok[0, t].astype(f32)) for t in range(n_tp)], axis=1)
    mean = jnp.mean(tokens * tokens, axis=1, keepdims=True)
    gain = jnp.concatenate([ag[i:i + 1, :] for i in range(ag.shape[0])], axis=1)
    normed = (tokens * lax.rsqrt(mean + EPSILON) * gain).astype(bf)
    for c in proj:
        c.wait()
    queries = jnp.dot(normed, wq_v[...], preferred_element_type=f32)
    keyval = jnp.dot(normed, wkv_v[...], preferred_element_type=f32)
    q_s[...] = jnp.zeros_like(q_s)
    kvn_s[...] = jnp.zeros_like(kvn_s)
    low_lanes = lane < HEAD_SIZE
    for i in range(heads // 2):
        turned = rotate(queries[:, i * 128:(i + 1) * 128]).astype(bf).astype(f32)
        q_s[:, 2 * i, :] = jnp.where(low_lanes, turned, 0.0)
        q_s[:, 2 * i + 1, :] = jnp.where(low_lanes, pltpu.roll(turned, HEAD_SIZE, 1), 0.0)
    for g in range(kvh):
        both = keyval[:, g * 128:(g + 1) * 128]
        both = jnp.where(low_lanes, rotate(both), both).astype(bf).astype(f32)
        for h in range(g * group, (g + 1) * group):
            kvn_s[:, h, :] = both

    for c in kv_loads:
        c.wait()
    kv_send[...] = kv_v[slot]
    kv_copy = rcopy(kv_send, kv_recv, kv_send_sem, kv_recv_sem, partner)
    kv_copy.start()

    def own_request(r):
        return q_s[r], kvn_s[r], kv_v[r], kvh * jnp.where(rep == 0, len_s[0, r], len_s[1, r])

    GROUP = 8

    def step(i, carry):
        rs = [i * GROUP + j for j in range(GROUP)]
        for r, o in zip(rs, attend([own_request(r) for r in rs], bias_s[...])):
            ctx_s[r] = o
        return carry

    lax.fori_loop(0, n // GROUP - 1, step, 0)
    kv_copy.wait()
    rs = list(range(n - GROUP, n))
    limit = kvh * jnp.where(rep == 0, len_s[1, slot], len_s[0, slot])
    last = attend([own_request(r) for r in rs] + [(q_s[slot], kvn_s[slot], kv_recv[...], limit)], bias_s[...])
    for r, o in zip(rs, last):
        ctx_s[r] = o
    arrived = last[-1]

    blocks = []
    for i in range(heads // 2):
        even = jnp.where(moved, arrived[2 * i:2 * i + 1], ctx_s[:, 2 * i, :])
        odd = jnp.where(moved, arrived[2 * i + 1:2 * i + 2], ctx_s[:, 2 * i + 1, :])
        blocks.append(jnp.where(low_lanes, pltpu.roll(even, HEAD_SIZE, 1), odd))
    context = jnp.concatenate(blocks, axis=1).astype(bf)
    load_o.wait()
    partial = jnp.dot(context, wo_v[...], preferred_element_type=f32)
    part_send[...] = partial.astype(bf)
    for k in (1, 3, 2):
        send(part_send, part_recv.at[tp], part_send_sem.at[k], part_recv_sem.at[tp], {"tp": tc(k)})
    own_gu.wait()
    own_dn.wait()
    split(0)
    took(raw.at[1], wx_s.at[0], wx_r.at[0], partner)
    took(dn.at[1], wx_s.at[1], wx_r.at[1], partner)
    split(1)
    total = tokens + partial
    for k in (1, 3, 2):
        t = tc(k)
        took(part_recv.at[t], part_send_sem.at[k], part_recv_sem.at[t], {"tp": t})
        total = total + part_recv[t].astype(f32)
    mean = jnp.mean(total * total, axis=1, keepdims=True)
    gain = jnp.concatenate([mg[i:i + 1, :] for i in range(mg.shape[0])], axis=1)
    x = (total * lax.rsqrt(mean + EPSILON) * gain).astype(bf)
    cut = a - GATE_LANES
    ga[z, y, :, GATE_LANES:] = x[:, 0:cut]
    gb[z, y] = x[:, cut:]

    ORDER = (0, 1, 3, 2)
    REL = ((0, 1), (3, 2))
    AWAY = (1, 3, 2)
    for d in (0, 1):
        send(gb.at[z, y], gb.at[z, y], b1_s.at[d, 1], b1_r.at[d, 1], nbr[d])
    for k in AWAY:
        send(ga.at[z, y], ga.at[z, y], a1_s.at[k], a1_r.at[y], at(yc(k), z))
    for d in (0, 1):
        send(ga.at[z, y], ga.at[z, y], a2_s.at[d, 1, 0], a2_r.at[d, 1, 0], nbr[d])
    for k in AWAY:
        send(gb.at[z, y], gb.at[z, y], b2_s.at[0, k], b2_r.at[z, y], at(yc(k), z))
    own = jnp.zeros((n, width), f32)
    for t in range(n_tp):
        own = jnp.where(tp == t, total[:, t * width:(t + 1) * width], own)
    xf[n_tp] = own
    number = (rep * n_req + req, (1 - rep) * n_req + req)

    def compute(zs):
        rows_a = jnp.concatenate([ga[zz].reshape(NY * n, a) for zz in zs], axis=0)
        rows_b = jnp.concatenate([gb[zz].reshape(NY * n, b) for zz in zs], axis=0)
        table = rows_a[:, 0:GATE_LANES].astype(f32)
        which = lax.rem(lax.broadcasted_iota(jnp.int32, table.shape, 1), GATE_LANES // 2)
        acts = []
        for j in (0, 1):
            weight = jnp.sum(jnp.where(which == number[j], table, 0.0), axis=1, keepdims=True)
            pr = jnp.dot(rows_a[:, GATE_LANES:], gu[j, 0:cut, :], preferred_element_type=f32)
            pr = pr + jnp.dot(rows_b, gu[j, cut:cut + b, :], preferred_element_type=f32)
            g, u = pr[:, 0:128], pr[:, 128:256]
            acts.append((g / (1.0 + jnp.exp(-g)) * u * weight).astype(bf))
        o = jnp.dot(acts[0], dn[0], preferred_element_type=f32) + jnp.dot(acts[1], dn[1], preferred_element_type=f32)
        for i, zz in enumerate(zs):
            block = o[i * NY * n:(i + 1) * NY * n]
            pa[zz] = block[:, 0:fa].reshape(NY, n, fa)
            pb[zz] = block[:, fa:].reshape(NY, n, fb)
            by_s[zz] = block[:, fa:].astype(bf).reshape(NY, n, fb)
            for k in AWAY:
                send(by_s.at[zz, yc(k)], by_r.at[zz, y], rby_s.at[zz, k], rby_r.at[zz, y], at(yc(k), z))

    def chunks(*steps):
        zs = []
        for s in steps:
            zs += [zc(s)] if s in (0, opp) else [zc(-s), zc(s)]
        for zz in zs:
            for k in AWAY:
                took(gb.at[zz, yc(k)], b2_s.at[0, k], b2_r.at[zz, yc(k)], at(yc(k), z))
        compute(zs)

    def a_send(d, k, i, value):
        sa[d, k, i] = value.astype(bf)
        send(sa.at[d, k, i], ra.at[d, k, i], rsa_s.at[d, k, i], rsa_r.at[d, k, i], nbr[d])

    def a_took(d, k, i):
        took(ra.at[d, k, i], rsa_s.at[d, k, i], rsa_r.at[d, k, i], nbr[d])
        return ra[d, k, i].astype(f32)

    def pass_b(s):
        for d in (0, 1):
            zz = zc(-s) if d == 0 else zc(s)
            if s < opp:
                took(gb.at[zz, y], b1_s.at[d, s], b1_r.at[d, s], nbr[d])
                block = gb.at[zz, y] if s + 1 < opp else gb.at[zz, y, :, part_b[d]]
                send(block, block, b1_s.at[d, s + 1], b1_r.at[d, s + 1], nbr[d])
            else:
                took(gb.at[zz, y, :, part_b[d]], b1_s.at[d, s], b1_r.at[d, s], nbr[d])
        for d in (0, 1) if s < opp else (0,):
            zz = zc(-s) if d == 0 else zc(s)
            for k in AWAY:
                send(gb.at[zz, y], gb.at[zz, y], b2_s.at[2 * s - 1 + d, k], b2_r.at[zz, y], at(yc(k), z))

    def pass_a(s):
        for i in ORDER:
            for d in (0, 1):
                if s == opp and i not in REL[d]:
                    continue
                zz = zc(-s) if d == 0 else zc(s)
                yb = yc(i)
                if s:
                    took(ga.at[zz, yb], a2_s.at[d, s, i], a2_r.at[d, s, i], nbr[d])
                elif i == 0:
                    continue
                elif d == 0:
                    took(ga.at[z, yb], a1_s.at[i], a1_r.at[yb], at(yb, z))
                if s + 1 < opp or (s + 1 == opp and i in REL[d]):
                    send(ga.at[zz, yb], ga.at[zz, yb], a2_s.at[d, s + 1, i], a2_r.at[d, s + 1, i], nbr[d])

    pass_b(1)
    pass_a(0)
    pass_b(2)
    pass_a(1)
    pass_b(3)
    pass_a(2)
    pass_b(4)
    chunks(0, 1)
    pass_a(3)
    chunks(2, 3)
    for d in (0, 1):
        for i in REL[1 - d]:
            a_send(d, opp - 1, i, pa[zc(opp - 1) if d == 0 else zc(1 - opp), yc(i)])
    pass_a(4)
    chunks(4)

    def a_step(k):
        for i in ORDER:
            for d in (0, 1):
                if k >= opp - 1 and i not in REL[d]:
                    continue
                value = pa[zc(k) if d == 0 else zc(-k), yc(i)]
                if k < opp:
                    value = value + a_took(d, k + 1, i)
                a_send(d, k, i, value)

    def b_own(zz):
        value = pb[zz, y]
        for k in AWAY:
            took(by_r.at[zz, yc(k)], rby_s.at[zz, k], rby_r.at[zz, yc(k)], at(yc(k), z))
            value = value + by_r[zz, yc(k)].astype(f32)
        return value

    def b_step(k):
        if k == opp:
            value = b_own(zc(k)).astype(bf)
            for d in (0, 1):
                lanes = part_fb[d]
                sb[d, k, :, lanes] = value[:, lanes]
                send(sb.at[d, k, :, lanes], rb.at[d, k, :, lanes], rsb_s.at[d, k], rsb_r.at[d, k], nbr[d])
            return
        for d in (0, 1):
            value = b_own(zc(k) if d == 0 else zc(-k))
            if k == opp - 1:
                lanes = part_fb[d]
                took(rb.at[d, k + 1, :, lanes], rsb_s.at[d, k + 1], rsb_r.at[d, k + 1], nbr[d])
                added = value[:, lanes] + rb[d, k + 1, :, lanes].astype(f32)
                value = jnp.concatenate([added, value[:, part_fb[1]]] if d == 0 else [value[:, part_fb[0]], added], axis=1)
            else:
                took(rb.at[d, k + 1], rsb_s.at[d, k + 1], rsb_r.at[d, k + 1], nbr[d])
                value = value + rb[d, k + 1].astype(f32)
            sb[d, k] = value.astype(bf)
            send(sb.at[d, k], rb.at[d, k], rsb_s.at[d, k], rsb_r.at[d, k], nbr[d])

    a_step(4)
    a_step(3)
    b_step(4)
    a_step(2)
    b_step(3)
    a_step(1)
    b_step(2)
    for k in AWAY:
        yb = yc(k)
        ys[yb] = (pa[z, yb] + a_took(0, 1, k) + a_took(1, 1, k)).astype(bf)
        send(ys.at[yb], yr.at[y], ry_s.at[k], ry_r.at[y], at(yb, z))
    total_a = pa[z, y] + a_took(0, 1, 0) + a_took(1, 1, 0)
    b_step(1)
    total_b = b_own(z)
    for d in (0, 1):
        took(rb.at[d, 1], rsb_s.at[d, 1], rsb_r.at[d, 1], nbr[d])
        total_b = total_b + rb[d, 1].astype(f32)
    for k in AWAY:
        yb = yc(k)
        took(yr.at[yb], ry_s.at[k], ry_r.at[yb], at(yb, z))
        total_a = total_a + yr[yb].astype(f32)

    total = jnp.concatenate([total_a, total_b], axis=1)
    for t in range(n_tp):
        quarter = total[:, t * width:(t + 1) * width]
        xf[t] = quarter
        xs[t] = quarter.astype(bf)
    for k in AWAY:
        t = tc(k)
        send(xs.at[t], xr.at[tp], rx_s.at[k], rx_r.at[tp], {"tp": t})
    value = xf[n_tp] + xf[tp]
    for k in AWAY:
        t = tc(k)
        took(xr.at[t], rx_s.at[k], rx_r.at[t], {"tp": t})
        value = value + xr[t].astype(f32)
    out[...] = value.astype(bf)
    for c in pending:
        c.wait_send()


def layer(
    hidden, lengths, migrate, kv_cache, attn_gain, moe_gain, w_query, key_value_weight, output_weight,
    w_gateup, w_down, expert_ids, expert_gates,
):
    n_tp, n_req = lax.axis_size("tp"), lax.axis_size("req")
    n, width = hidden.shape
    model = w_query.shape[0]
    kvh = kv_cache.shape[2]
    kv = kv_cache.reshape(n, kv_cache.shape[1] * kvh, kv_cache.shape[3])
    lanes = kv.shape[1]
    i = np.arange(128) % (HEAD_SIZE // 2)
    freq = jnp.asarray((ROPE_BASE ** (-2.0 * i / HEAD_SIZE)).astype(np.float32)[None])
    ag, mg = attn_gain.reshape(-1, 128), moe_gain.reshape(-1, 128)
    ids, gates = expert_ids.T, expert_gates.T
    a, fa = A_LANES, FA_LANES
    b, fb = GATE_LANES + model - a, model - fa
    gu = w_gateup.reshape(2 * model, w_gateup.shape[3])
    dn = w_down[0]
    bf, f32 = jnp.bfloat16, jnp.float32
    dma, v = pltpu.SemaphoreType.DMA, pltpu.VMEM
    k5 = NZ // 2 + 1
    args = (lengths, migrate, hidden, kv, ag, mg, freq, w_query, key_value_weight, output_weight, ids, gates, gu, dn)
    return pl.pallas_call(
        functools.partial(layer_kernel, n_tp, n_req),
        name="layer",
        out_shape=jax.ShapeDtypeStruct((n, width), bf),
        in_specs=[pl.BlockSpec(memory_space=pltpu.SMEM if i == 1 else pltpu.HBM) for i in range(len(args))],
        out_specs=pl.BlockSpec(memory_space=pltpu.VMEM),
        scratch_shapes=[
            pltpu.SMEM(lengths.shape, jnp.int32),
            v(hidden.shape, bf), v(ag.shape, f32), v(mg.shape, f32), v(freq.shape, f32), v(ids.shape, jnp.int32), v(gates.shape, f32),
            v(kv.shape, bf), v(w_query.shape, bf), v(key_value_weight.shape, bf), v(output_weight.shape, bf),
            v((2, n_tp, n, width), bf), v(kv.shape[1:], bf), v(kv.shape[1:], bf), v((n, model), bf), v((n_tp, n, model), bf),
            v((n, 8, 128), f32), v((n, 8, 128), f32), v((n, 8, 128), f32), v((8, lanes), f32),
            v((NZ, NY, n, a), bf), v((NZ, NY, n, b), bf), v((NZ, NY, n, fa), f32), v((NZ, NY, n, fb), f32),
            v((2,) + gu.shape, bf), v((512, 128), f32), v((2, model, 256), bf), v((2,) + dn.shape, bf),
            v((NZ, NY, n, fb), bf), v((NZ, NY, n, fb), bf),
            v((2, k5, NY, n, fa), bf), v((2, k5, NY, n, fa), bf), v((2, k5, n, fb), bf), v((2, k5, n, fb), bf),
            v((NY, n, fa), bf), v((NY, n, fa), bf), v((n_tp, n, width), bf), v((n_tp, n, width), bf), v((n_tp + 1, n, width), f32),
            dma((16,)), dma((n,)), dma((2 * n_tp,)), dma((2, n_tp)), dma, dma, dma((n_tp,)), dma((n_tp,)),
            dma((2,)), dma((2,)), dma((NY,)), dma((NY,)), dma((2, k5, NY)), dma((2, k5, NY)), dma((2, k5)), dma((2, k5)),
            dma((NZ, NY)), dma((NZ, NY)),
            dma((NZ, NY)), dma((NZ, NY)), dma((2, k5, NY)), dma((2, k5, NY)), dma((2, k5)), dma((2, k5)), dma((NY,)), dma((NY,)),
            dma((n_tp,)), dma((n_tp,)),
        ],
        compiler_params=pltpu.CompilerParams(collective_id=0, has_side_effects=True, vmem_limit_bytes=VMEM_LIMIT),
        cost_estimate=pl.CostEstimate(flops=1_500_000_000, bytes_accessed=16_000_000, transcendentals=1_000_000),
    )(*args)


def solution(mesh):
    placed = (
        P(("rep", "req"), "tp"),
        P(None, "req"),
        P("req"),
        P(("rep", "req"), None, "tp", None),
        P(),
        P(),
        P(None, "tp"),
        P(None, "tp"),
        P("tp", None),
        P(("rep", "req"), None, None, "tp"),
        P(("rep", "req"), "tp", None),
        P(("rep", "req"), None),
        P(("rep", "req"), None),
    )
    return jax.shard_map(
        layer, mesh=mesh, in_specs=placed, out_specs=P(("rep", "req"), "tp"), check_vma=False
    )
```

```python
import functools
import jax
import jax.numpy as jnp
import numpy as np
from jax import lax
from jax.experimental import pallas as pl
from jax.experimental.pallas import tpu as pltpu
from jax.sharding import PartitionSpec as P

MESH = pl.DeviceIdType.MESH
HEAD_SIZE = 64
EPSILON = 1e-06
ROPE_BASE = 10000.0
MASKED = -1e30
GATE_LANES = 128
NY, NZ = 4, 8
VMEM_LIMIT = 58 * 2**20
A_LANES, FA_LANES = 896, 768


def rows_of(scalars, n):
    row = lax.broadcasted_iota(jnp.int32, (n, 128), 0)
    out = jnp.zeros((n, 128), jnp.int32)
    for r in range(n):
        out = jnp.where(row == r, scalars(r), out)
    return out


def attend(requests, bias):
    scale = HEAD_SIZE ** (-0.5)
    scores, owns = [], []
    for q, kvn, kv, limit in requests:
        s = lax.dot_general(q.astype(jnp.bfloat16), kv, (((1,), (1,)), ((), ())), preferred_element_type=jnp.float32)
        place = lax.broadcasted_iota(jnp.int32, s.shape, 1)
        scores.append(jnp.where(place < limit, s * scale + bias, MASKED)[None])
        owns.append((jnp.sum(q * kvn, axis=1, keepdims=True) * scale)[None])
    s, own = jnp.concatenate(scores, axis=0), jnp.concatenate(owns, axis=0)
    peak = jnp.maximum(jnp.max(s, axis=2, keepdims=True), own)
    p = jnp.exp(s - peak)
    p_own = jnp.exp(own - peak)
    inv = 1.0 / (jnp.sum(p, axis=2, keepdims=True) + p_own)
    w = (p * inv).astype(jnp.bfloat16)
    w_own = (p_own * inv).astype(jnp.bfloat16).astype(jnp.float32)
    return [jnp.dot(w[g], kv, preferred_element_type=jnp.float32) + w_own[g] * kvn for g, (q, kvn, kv, limit) in enumerate(requests)]


def layer_kernel(
    n_tp, n_req,
    len_h, mig_s, hid_h, kv_h, ag_h, mg_h, freq_h, wq_h, wkv_h, wo_h, ids_h, gates_h, gu_h, dn_h,
    out,
    len_s, hid, ag, mg, freq, ids, gates,
    kv_v, wq_v, wkv_v, wo_v, tok, kv_send, kv_recv, part_send, part_recv, q_s, kvn_s, ctx_s, bias_s,
    ga, gb, pa, pb, raw, wide, gu, dn,
    by_s, by_r, sa, ra, sb, rb, ys, yr, xs, xr, xf,
    load_sem, kv_sem, tok_send_sem, tok_recv_sem, kv_send_sem, kv_recv_sem, part_send_sem, part_recv_sem,
    wx_s, wx_r, a1_s, a1_r, a2_s, a2_r, b1_s, b1_r, b2_s, b2_r,
    rby_s, rby_r, rsa_s, rsa_r, rsb_s, rsb_r, ry_s, ry_r, rx_s, rx_r,
):
    rep, req, tp = lax.axis_index("rep"), lax.axis_index("req"), lax.axis_index("tp")
    y, z = req // NZ, lax.rem(req, NZ)
    n, width = hid.shape
    heads = wq_v.shape[1] // HEAD_SIZE
    kvh = wkv_v.shape[1] // (2 * HEAD_SIZE)
    group = heads // kvh
    n_lanes = kv_v.shape[1]
    a, b, fa, fb = ga.shape[-1], gb.shape[-1], pa.shape[-1], pb.shape[-1]
    opp = NZ // 2
    part_b = (slice(0, b // 256 * 128), slice(b // 256 * 128, b))
    part_fb = (slice(0, fb // 256 * 128), slice(fb // 256 * 128, fb))
    bf, f32 = jnp.bfloat16, jnp.float32

    def zc(k):
        return lax.rem(z + (k + NZ), NZ)

    def yc(k):
        return lax.rem(y + k, NY)

    def tc(k):
        return lax.rem(tp + k, n_tp)

    def at(yy, zz):
        return {"req": yy * NZ + zz}

    nbr = (at(y, zc(1)), at(y, zc(-1)))
    partner = {"rep": 1 - rep}

    def rcopy(src, dst, ssem, rsem, dev):
        return pltpu.make_async_remote_copy(src_ref=src, dst_ref=dst, send_sem=ssem, recv_sem=rsem, device_id=dev, device_id_type=MESH)

    def send(*args):
        rcopy(*args).start()

    def sent(blocks, ssem):
        rcopy(blocks, blocks, ssem, ssem, partner).wait_send()

    def took(dst, ssem, rsem, dev):
        rcopy(dst, dst, ssem, rsem, dev).wait_recv()

    loads = []

    def load(src, dst):
        c = pltpu.make_async_copy(src, dst, load_sem.at[len(loads)])
        c.start()
        loads.append(c)
        return c

    small = [load(*p) for p in ((hid_h, hid), (len_h, len_s), (ids_h, ids), (gates_h, gates), (freq_h, freq), (ag_h, ag), (mg_h, mg))]
    proj = [load(wq_h, wq_v), load(wkv_h, wkv_v)]
    for r in range(n):
        pltpu.make_async_copy(kv_h.at[r], kv_v.at[r], kv_sem).start()
    load_o = load(wo_h, wo_v)
    own_gu = load(gu_h, raw.at[0])
    own_dn = load(dn_h, dn.at[0])

    barrier = pltpu.get_barrier_semaphore()
    peers = [(0, tc(k)) for k in range(1, n_tp)] + [(1, tc(k)) for k in range(n_tp)]
    far_rep = lambda side: rep if side == 0 else 1 - rep
    greet = [{"rep": far_rep(side), "tp": t} for side, t in peers]
    greet += [at(yc(k), z) for k in range(1, NY)] + [nbr[0], nbr[1]]
    for dev in greet:
        pl.semaphore_signal(barrier, inc=1, device_id=dev, device_id_type=MESH)
    pl.semaphore_wait(barrier, len(greet))

    for c in small:
        c.wait()
    for side, t in peers:
        send(hid, tok.at[side, tp], tok_send_sem.at[side], tok_recv_sem.at[side], {"rep": far_rep(side), "tp": t})
    tok[0, tp] = hid[...]
    send(gu_h, raw.at[1], wx_s.at[0], wx_r.at[0], partner)
    send(dn_h, dn.at[1], wx_s.at[1], wx_r.at[1], partner)

    slot = mig_s[0]
    row = lax.broadcasted_iota(jnp.int32, (n, 128), 0)
    lane = lax.broadcasted_iota(jnp.int32, (n, 128), 1)
    moved = row == slot
    own_span = rows_of(lambda r: jnp.where(rep == 0, len_s[0, r], len_s[1, r]), n)
    other_span = rows_of(lambda r: jnp.where(rep == 0, len_s[1, r], len_s[0, r]), n)
    span = jnp.where(moved, other_span, own_span).astype(f32)
    angle = span * freq[...]
    cosine, sine = jnp.cos(angle), jnp.sin(angle)
    first = lax.rem(lane, HEAD_SIZE) < HEAD_SIZE // 2
    half = HEAD_SIZE // 2

    def rotate(v):
        turned = jnp.where(first, -pltpu.roll(v, 128 - half, 1), pltpu.roll(v, half, 1))
        return v * cosine + turned * sine

    head = lax.broadcasted_iota(jnp.int32, bias_s.shape, 0)
    pos = lax.broadcasted_iota(jnp.int32, bias_s.shape, 1)
    bias_s[...] = jnp.where(lax.rem(pos, kvh) == head // group, 0.0, MASKED)

    eye = lax.broadcasted_iota(jnp.int32, (n, n), 0) == lax.broadcasted_iota(jnp.int32, (n, n), 1)
    expert = lax.rem(lane, GATE_LANES // 2)
    dense = jnp.zeros((n, 128), f32)
    for k in range(ids.shape[0]):
        idc = jnp.sum(jnp.where(eye, ids[k:k + 1, :], 0), axis=1, keepdims=True)
        gc = jnp.sum(jnp.where(eye, gates[k:k + 1, :], 0.0), axis=1, keepdims=True)
        dense = dense + jnp.where(expert == idc, gc, 0.0)
    high = dense.astype(bf).astype(f32)
    ga[z, y, :, 0:GATE_LANES] = jnp.where(lane < GATE_LANES // 2, high, dense - high).astype(bf)

    part = wide.shape[0]

    def split(j):
        def step(i, carry):
            start = pl.multiple_of(i * part, part)
            wide[...] = raw[j, pl.ds(start, part), :].astype(f32)
            rows = pl.ds(pl.multiple_of(i * (part // 2), part // 2), part // 2)
            gu[j, rows, 0:128] = wide[pl.ds(0, part // 2, stride=2), :].astype(bf)
            gu[j, rows, 128:256] = wide[pl.ds(1, part // 2, stride=2), :].astype(bf)
            return carry
        lax.fori_loop(0, raw.shape[1] // part, step, 0)

    took(tok.at[0, 0:n_tp - 1], tok_send_sem.at[0], tok_recv_sem.at[0], partner)
    took(tok.at[1], tok_send_sem.at[1], tok_recv_sem.at[1], partner)

    moved_w = lax.broadcasted_iota(jnp.int32, (n, width), 0) == slot
    tokens = jnp.concatenate(
        [jnp.where(moved_w, tok[1, t].astype(f32), tok[0, t].astype(f32)) for t in range(n_tp)], axis=1)
    mean = jnp.mean(tokens * tokens, axis=1, keepdims=True)
    gain = jnp.concatenate([ag[i:i + 1, :] for i in range(ag.shape[0])], axis=1)
    normed = (tokens * lax.rsqrt(mean + EPSILON) * gain).astype(bf)
    for c in proj:
        c.wait()
    queries = jnp.dot(normed, wq_v[...], preferred_element_type=f32)
    keyval = jnp.dot(normed, wkv_v[...], preferred_element_type=f32)
    q_s[...] = jnp.zeros_like(q_s)
    kvn_s[...] = jnp.zeros_like(kvn_s)
    low_lanes = lane < HEAD_SIZE
    for i in range(heads // 2):
        turned = rotate(queries[:, i * 128:(i + 1) * 128]).astype(bf).astype(f32)
        q_s[:, 2 * i, :] = jnp.where(low_lanes, turned, 0.0)
        q_s[:, 2 * i + 1, :] = jnp.where(low_lanes, pltpu.roll(turned, HEAD_SIZE, 1), 0.0)
    for g in range(kvh):
        both = keyval[:, g * 128:(g + 1) * 128]
        both = jnp.where(low_lanes, rotate(both), both).astype(bf).astype(f32)
        for h in range(g * group, (g + 1) * group):
            kvn_s[:, h, :] = both

    pltpu.make_async_copy(kv_h, kv_v, kv_sem).wait()
    kv_send[...] = kv_v[slot]
    kv_copy = rcopy(kv_send, kv_recv, kv_send_sem, kv_recv_sem, partner)
    kv_copy.start()

    def own_request(r):
        return q_s[r], kvn_s[r], kv_v[r], kvh * jnp.where(rep == 0, len_s[0, r], len_s[1, r])

    GROUP = 8

    def step(i, carry):
        rs = [i * GROUP + j for j in range(GROUP)]
        for r, o in zip(rs, attend([own_request(r) for r in rs], bias_s[...])):
            ctx_s[r] = o
        return carry

    lax.fori_loop(0, n // GROUP - 1, step, 0)
    kv_copy.wait()
    rs = list(range(n - GROUP, n))
    limit = kvh * jnp.where(rep == 0, len_s[1, slot], len_s[0, slot])
    last = attend([own_request(r) for r in rs] + [(q_s[slot], kvn_s[slot], kv_recv[...], limit)], bias_s[...])
    for r, o in zip(rs, last):
        ctx_s[r] = o
    arrived = last[-1]

    blocks = []
    for i in range(heads // 2):
        even = jnp.where(moved, arrived[2 * i:2 * i + 1], ctx_s[:, 2 * i, :])
        odd = jnp.where(moved, arrived[2 * i + 1:2 * i + 2], ctx_s[:, 2 * i + 1, :])
        blocks.append(jnp.where(low_lanes, pltpu.roll(even, HEAD_SIZE, 1), odd))
    context = jnp.concatenate(blocks, axis=1).astype(bf)
    load_o.wait()
    partial = jnp.dot(context, wo_v[...], preferred_element_type=f32)
    part_send[...] = partial.astype(bf)
    for k in (1, 3, 2):
        send(part_send, part_recv.at[tp], part_send_sem, part_recv_sem, {"tp": tc(k)})
    own_gu.wait()
    own_dn.wait()
    split(0)
    took(raw.at[1], wx_s.at[0], wx_r.at[0], partner)
    took(dn.at[1], wx_s.at[1], wx_r.at[1], partner)
    split(1)
    total = tokens + partial
    took(part_recv.at[0:n_tp - 1], part_send_sem, part_recv_sem, partner)
    for k in (1, 3, 2):
        total = total + part_recv[tc(k)].astype(f32)
    mean = jnp.mean(total * total, axis=1, keepdims=True)
    gain = jnp.concatenate([mg[i:i + 1, :] for i in range(mg.shape[0])], axis=1)
    x = (total * lax.rsqrt(mean + EPSILON) * gain).astype(bf)
    cut = a - GATE_LANES
    ga[z, y, :, GATE_LANES:] = x[:, 0:cut]
    gb[z, y] = x[:, cut:]

    ORDER = (0, 1, 3, 2)
    REL = ((0, 1), (3, 2))
    AWAY = (1, 3, 2)
    for d in (0, 1):
        send(gb.at[z, y], gb.at[z, y], b1_s.at[0], b1_r.at[d, 1], nbr[d])
    for k in AWAY:
        send(ga.at[z, y], ga.at[z, y], a1_s, a1_r.at[y], at(yc(k), z))
    for d in (0, 1):
        send(ga.at[z, y], ga.at[z, y], a2_s, a2_r.at[d, 1, 0], nbr[d])
    for k in AWAY:
        send(gb.at[z, y], gb.at[z, y], b2_s, b2_r.at[z], at(yc(k), z))
    own = jnp.zeros((n, width), f32)
    for t in range(n_tp):
        own = jnp.where(tp == t, total[:, t * width:(t + 1) * width], own)
    xf[n_tp] = own
    number = (rep * n_req + req, (1 - rep) * n_req + req)

    def compute(zs):
        rows_a = jnp.concatenate([ga[zz].reshape(NY * n, a) for zz in zs], axis=0)
        rows_b = jnp.concatenate([gb[zz].reshape(NY * n, b) for zz in zs], axis=0)
        table = rows_a[:, 0:GATE_LANES].astype(f32)
        which = lax.rem(lax.broadcasted_iota(jnp.int32, table.shape, 1), GATE_LANES // 2)
        acts = []
        for j in (0, 1):
            weight = jnp.sum(jnp.where(which == number[j], table, 0.0), axis=1, keepdims=True)
            pr = jnp.dot(rows_a[:, GATE_LANES:], gu[j, 0:cut, :], preferred_element_type=f32)
            pr = pr + jnp.dot(rows_b, gu[j, cut:cut + b, :], preferred_element_type=f32)
            g, u = pr[:, 0:128], pr[:, 128:256]
            acts.append((g / (1.0 + jnp.exp(-g)) * u * weight).astype(bf))
        o = jnp.dot(acts[0], dn[0], preferred_element_type=f32) + jnp.dot(acts[1], dn[1], preferred_element_type=f32)
        for i, zz in enumerate(zs):
            block = o[i * NY * n:(i + 1) * NY * n]
            pa[zz] = block[:, 0:fa].reshape(NY, n, fa)
            pb[zz] = block[:, fa:].reshape(NY, n, fb)
            by_s[zz] = block[:, fa:].astype(bf).reshape(NY, n, fb)
            for k in AWAY:
                send(by_s.at[zz, yc(k)], by_r.at[zz, y], rby_s, rby_r.at[zz], at(yc(k), z))

    def chunks(*steps):
        zs = []
        for s in steps:
            zs += [zc(s)] if s in (0, opp) else [zc(-s), zc(s)]
        for zz in zs:
            took(gb.at[zz, 0:NY - 1], b2_s, b2_r.at[zz], partner)
        compute(zs)

    def a_send(d, k, i, value):
        sa[d * (opp + 1) + k, i] = value.astype(bf)
        send(sa.at[d * (opp + 1) + k, i], ra.at[d, k, i], rsa_s, rsa_r.at[d, k, i], nbr[d])

    def a_took(d, k, i):
        took(ra.at[d, k, i], rsa_s, rsa_r.at[d, k, i], nbr[d])
        return ra[d, k, i].astype(f32)

    def pass_b(s):
        for d in (0, 1):
            zz = zc(-s) if d == 0 else zc(s)
            if s < opp:
                took(gb.at[zz, y], b1_s.at[0], b1_r.at[d, s], nbr[d])
                block = gb.at[zz, y] if s + 1 < opp else gb.at[zz, y, :, part_b[d]]
                send(block, block, b1_s.at[0 if s + 1 < opp else 1], b1_r.at[d, s + 1], nbr[d])
            else:
                took(gb.at[zz, y, :, part_b[d]], b1_s.at[0], b1_r.at[d, s], nbr[d])
        for d in (0, 1) if s < opp else (0,):
            zz = zc(-s) if d == 0 else zc(s)
            for k in AWAY:
                send(gb.at[zz, y], gb.at[zz, y], b2_s, b2_r.at[zz], at(yc(k), z))

    def pass_a(s):
        for i in ORDER:
            for d in (0, 1):
                if s == opp and i not in REL[d]:
                    continue
                zz = zc(-s) if d == 0 else zc(s)
                yb = yc(i)
                if s:
                    took(ga.at[zz, yb], a2_s, a2_r.at[d, s, i], nbr[d])
                elif i == 0:
                    continue
                elif d == 0:
                    took(ga.at[z, yb], a1_s, a1_r.at[yb], at(yb, z))
                if s + 1 < opp or (s + 1 == opp and i in REL[d]):
                    send(ga.at[zz, yb], ga.at[zz, yb], a2_s, a2_r.at[d, s + 1, i], nbr[d])

    pass_b(1)
    pass_a(0)
    pass_b(2)
    pass_a(1)
    pass_b(3)
    pass_a(2)
    pass_b(4)
    chunks(0, 1)
    pass_a(3)
    chunks(2, 3)
    for d in (0, 1):
        for i in REL[1 - d]:
            a_send(d, opp - 1, i, pa[zc(opp - 1) if d == 0 else zc(1 - opp), yc(i)])
    pass_a(4)
    chunks(4)

    def a_step(k):
        for i in ORDER:
            for d in (0, 1):
                if k >= opp - 1 and i not in REL[d]:
                    continue
                value = pa[zc(k) if d == 0 else zc(-k), yc(i)]
                if k < opp:
                    value = value + a_took(d, k + 1, i)
                a_send(d, k, i, value)

    def b_own(zz):
        value = pb[zz, y]
        took(by_r.at[zz, 0:NY - 1], rby_s, rby_r.at[zz], partner)
        for k in AWAY:
            value = value + by_r[zz, yc(k)].astype(f32)
        return value

    def b_step(k):
        if k == opp:
            value = b_own(zc(k)).astype(bf)
            for d in (0, 1):
                lanes = part_fb[d]
                sb[d, k, :, lanes] = value[:, lanes]
                send(sb.at[d, k, :, lanes], rb.at[d, k, :, lanes], rsb_s.at[1], rsb_r.at[d, k], nbr[d])
            return
        for d in (0, 1):
            value = b_own(zc(k) if d == 0 else zc(-k))
            if k == opp - 1:
                lanes = part_fb[d]
                took(rb.at[d, k + 1, :, lanes], rsb_s.at[0], rsb_r.at[d, k + 1], nbr[d])
                added = value[:, lanes] + rb[d, k + 1, :, lanes].astype(f32)
                value = jnp.concatenate([added, value[:, part_fb[1]]] if d == 0 else [value[:, part_fb[0]], added], axis=1)
            else:
                took(rb.at[d, k + 1], rsb_s.at[0], rsb_r.at[d, k + 1], nbr[d])
                value = value + rb[d, k + 1].astype(f32)
            sb[d, k] = value.astype(bf)
            send(sb.at[d, k], rb.at[d, k], rsb_s.at[0], rsb_r.at[d, k], nbr[d])

    a_step(4)
    a_step(3)
    b_step(4)
    a_step(2)
    b_step(3)
    a_step(1)
    b_step(2)
    for k in AWAY:
        yb = yc(k)
        ys[yb] = (pa[z, yb] + a_took(0, 1, k) + a_took(1, 1, k)).astype(bf)
        send(ys.at[yb], yr.at[y], ry_s, ry_r, at(yb, z))
    total_a = pa[z, y] + a_took(0, 1, 0) + a_took(1, 1, 0)
    b_step(1)
    total_b = b_own(z)
    for d in (0, 1):
        took(rb.at[d, 1], rsb_s.at[0], rsb_r.at[d, 1], nbr[d])
        total_b = total_b + rb[d, 1].astype(f32)
    took(yr.at[0:NY - 1], ry_s, ry_r, partner)
    for k in AWAY:
        total_a = total_a + yr[yc(k)].astype(f32)

    total = jnp.concatenate([total_a, total_b], axis=1)
    for t in range(n_tp):
        quarter = total[:, t * width:(t + 1) * width]
        xf[t] = quarter
        xs[t] = quarter.astype(bf)
    for k in AWAY:
        t = tc(k)
        send(xs.at[t], xr.at[tp], rx_s, rx_r, {"tp": t})
    value = xf[n_tp] + xf[tp]
    took(xr.at[0:n_tp - 1], rx_s, rx_r, partner)
    for k in AWAY:
        value = value + xr[tc(k)].astype(f32)
    out[...] = value.astype(bf)
    sent(tok.at[0, 0:n_tp - 1], tok_send_sem.at[0])
    sent(tok.at[1], tok_send_sem.at[1])
    sent(raw.at[0], wx_s.at[0])
    sent(dn.at[0], wx_s.at[1])
    sent(part_recv.at[0:n_tp - 1], part_send_sem)
    sent(ga.at[0, 0:NY - 1], a1_s)
    sent(ga.at[0:NZ - 1], a2_s)
    sent(gb.at[0:opp - 1, 0:2], b1_s.at[0])
    sent(gb.at[0, 0], b1_s.at[1])
    sent(gb.at[0:NZ - 2], b2_s)
    sent(by_s.at[0:NZ - 2], rby_s)
    sent(sa.at[0:NZ - 1], rsa_s)
    sent(sb.at[:, 0:opp - 1], rsb_s.at[0])
    sent(sb.at[0, 0], rsb_s.at[1])
    sent(ys.at[0:NY - 1], ry_s)
    sent(xs.at[0:n_tp - 1], rx_s)


def layer(
    hidden, lengths, migrate, kv_cache, attn_gain, moe_gain, w_query, key_value_weight, output_weight,
    w_gateup, w_down, expert_ids, expert_gates,
):
    n_tp, n_req = lax.axis_size("tp"), lax.axis_size("req")
    n, width = hidden.shape
    model = w_query.shape[0]
    kvh = kv_cache.shape[2]
    kv = kv_cache.reshape(n, kv_cache.shape[1] * kvh, kv_cache.shape[3])
    lanes = kv.shape[1]
    i = np.arange(128) % (HEAD_SIZE // 2)
    freq = jnp.asarray((ROPE_BASE ** (-2.0 * i / HEAD_SIZE)).astype(np.float32)[None])
    ag, mg = attn_gain.reshape(-1, 128), moe_gain.reshape(-1, 128)
    ids, gates = expert_ids.T, expert_gates.T
    a, fa = A_LANES, FA_LANES
    b, fb = GATE_LANES + model - a, model - fa
    gu = w_gateup.reshape(2 * model, w_gateup.shape[3])
    dn = w_down[0]
    bf, f32 = jnp.bfloat16, jnp.float32
    dma, v = pltpu.SemaphoreType.DMA, pltpu.VMEM
    k5 = NZ // 2 + 1
    args = (lengths, migrate, hidden, kv, ag, mg, freq, w_query, key_value_weight, output_weight, ids, gates, gu, dn)
    return pl.pallas_call(
        functools.partial(layer_kernel, n_tp, n_req),
        name="layer",
        out_shape=jax.ShapeDtypeStruct((n, width), bf),
        in_specs=[pl.BlockSpec(memory_space=pltpu.SMEM if i == 1 else pltpu.HBM) for i in range(len(args))],
        out_specs=pl.BlockSpec(memory_space=pltpu.VMEM),
        scratch_shapes=[
            pltpu.SMEM(lengths.shape, jnp.int32),
            v(hidden.shape, bf), v(ag.shape, f32), v(mg.shape, f32), v(freq.shape, f32), v(ids.shape, jnp.int32), v(gates.shape, f32),
            v(kv.shape, bf), v(w_query.shape, bf), v(key_value_weight.shape, bf), v(output_weight.shape, bf),
            v((2, n_tp, n, width), bf), v(kv.shape[1:], bf), v(kv.shape[1:], bf), v((n, model), bf), v((n_tp, n, model), bf),
            v((n, 8, 128), f32), v((n, 8, 128), f32), v((n, 8, 128), f32), v((8, lanes), f32),
            v((NZ, NY, n, a), bf), v((NZ, NY, n, b), bf), v((NZ, NY, n, fa), f32), v((NZ, NY, n, fb), f32),
            v((2,) + gu.shape, bf), v((512, 128), f32), v((2, model, 256), bf), v((2,) + dn.shape, bf),
            v((NZ, NY, n, fb), bf), v((NZ, NY, n, fb), bf),
            v((2 * k5, NY, n, fa), bf), v((2, k5, NY, n, fa), bf), v((2, k5, n, fb), bf), v((2, k5, n, fb), bf),
            v((NY, n, fa), bf), v((NY, n, fa), bf), v((n_tp, n, width), bf), v((n_tp, n, width), bf), v((n_tp + 1, n, width), f32),
            dma((12,)), dma, dma((2,)), dma((2,)), dma, dma, dma, dma,
            dma((2,)), dma((2,)), dma, dma((NY,)), dma, dma((2, k5, NY)), dma((2,)), dma((2, k5)), dma, dma((NZ,)),
            dma, dma((NZ,)), dma, dma((2, k5, NY)), dma((2,)), dma((2, k5)), dma, dma, dma, dma,
        ],
        compiler_params=pltpu.CompilerParams(collective_id=0, has_side_effects=True, vmem_limit_bytes=VMEM_LIMIT),
        cost_estimate=pl.CostEstimate(flops=1_500_000_000, bytes_accessed=16_000_000, transcendentals=1_000_000),
    )(*args)


def solution(mesh):
    placed = (
        P(("rep", "req"), "tp"),
        P(None, "req"),
        P("req"),
        P(("rep", "req"), None, "tp", None),
        P(),
        P(),
        P(None, "tp"),
        P(None, "tp"),
        P("tp", None),
        P(("rep", "req"), None, None, "tp"),
        P(("rep", "req"), "tp", None),
        P(("rep", "req"), None),
        P(("rep", "req"), None),
    )
    return jax.shard_map(
        layer, mesh=mesh, in_specs=placed, out_specs=P(("rep", "req"), "tp"), check_vma=False
    )
```

```python
import functools
import jax
import jax.numpy as jnp
import numpy as np
from jax import lax
from jax.experimental import pallas as pl
from jax.experimental.pallas import tpu as pltpu
from jax.sharding import PartitionSpec as P

MESH = pl.DeviceIdType.MESH
HEAD_SIZE = 64
EPSILON = 1e-06
ROPE_BASE = 10000.0
MASKED = -1e30
GATE_LANES = 128
NY, NZ = 4, 8
VMEM_LIMIT = 58 * 2**20
A_LANES, FA_LANES = 896, 768


def rows_of(scalars, n):
    row = lax.broadcasted_iota(jnp.int32, (n, 128), 0)
    out = jnp.zeros((n, 128), jnp.int32)
    for r in range(n):
        out = jnp.where(row == r, scalars(r), out)
    return out


def attend(requests, bias):
    scale = HEAD_SIZE ** (-0.5)
    scores, owns = [], []
    for q, kvn, kv, limit in requests:
        s = lax.dot_general(q.astype(jnp.bfloat16), kv, (((1,), (1,)), ((), ())), preferred_element_type=jnp.float32)
        place = lax.broadcasted_iota(jnp.int32, s.shape, 1)
        scores.append(jnp.where(place < limit, s * scale + bias, MASKED)[None])
        owns.append((jnp.sum(q * kvn, axis=1, keepdims=True) * scale)[None])
    s, own = jnp.concatenate(scores, axis=0), jnp.concatenate(owns, axis=0)
    peak = jnp.maximum(jnp.max(s, axis=2, keepdims=True), own)
    p = jnp.exp(s - peak)
    p_own = jnp.exp(own - peak)
    inv = 1.0 / (jnp.sum(p, axis=2, keepdims=True) + p_own)
    w = (p * inv).astype(jnp.bfloat16)
    w_own = (p_own * inv).astype(jnp.bfloat16).astype(jnp.float32)
    return [jnp.dot(w[g], kv, preferred_element_type=jnp.float32) + w_own[g] * kvn for g, (q, kvn, kv, limit) in enumerate(requests)]


def layer_kernel(
    n_tp, n_req,
    len_h, mig_s, hid_h, kv_h, ag_h, mg_h, freq_h, wq_h, wkv_h, wo_h, ids_h, gates_h, gu_h, dn_h,
    out,
    len_s, hid, ag, mg, freq, ids, gates,
    kv_v, wq_v, wkv_v, wo_v, tok, kv_send, kv_recv, part_send, part_recv, q_s, kvn_s, ctx_s, bias_s,
    ga, gb, pa, pb, raw, wide, gu, dn,
    by_s, by_r, sa, ra, sb, rb, ys, yr, xs, xr, xf,
    load_sem, kv_sem, tok_send_sem, tok_recv_sem, kv_send_sem, kv_recv_sem, part_send_sem, part_recv_sem,
    wx_s, wx_r, a1_s, a1_r, a2_s, a2_r, b1_s, b1_r, b2_s, b2_r,
    rby_s, rby_r, rsa_s, rsa_r, rsb_s, rsb_r, ry_s, ry_r, rx_s, rx_r,
):
    rep, req, tp = lax.axis_index("rep"), lax.axis_index("req"), lax.axis_index("tp")
    y, z = req // NZ, lax.rem(req, NZ)
    n, width = hid.shape
    heads = wq_v.shape[1] // HEAD_SIZE
    kvh = wkv_v.shape[1] // (2 * HEAD_SIZE)
    group = heads // kvh
    n_lanes = kv_v.shape[1]
    a, b, fa, fb = ga.shape[-1], gb.shape[-1], pa.shape[-1], pb.shape[-1]
    opp = NZ // 2
    part_b = (slice(0, b // 256 * 128), slice(b // 256 * 128, b))
    part_fb = (slice(0, fb // 256 * 128), slice(fb // 256 * 128, fb))
    bf, f32 = jnp.bfloat16, jnp.float32

    def zc(k):
        return lax.rem(z + (k + NZ), NZ)

    def yc(k):
        return lax.rem(y + k, NY)

    def tc(k):
        return lax.rem(tp + k, n_tp)

    def at(yy, zz):
        return {"req": yy * NZ + zz}

    nbr = (at(y, zc(1)), at(y, zc(-1)))
    partner = {"rep": 1 - rep}

    def rcopy(src, dst, ssem, rsem, dev):
        return pltpu.make_async_remote_copy(src_ref=src, dst_ref=dst, send_sem=ssem, recv_sem=rsem, device_id=dev, device_id_type=MESH)

    def send(*args):
        rcopy(*args).start()

    def sent(blocks, ssem):
        rcopy(blocks, blocks, ssem, ssem, partner).wait_send()

    def took(dst, ssem, rsem, dev):
        rcopy(dst, dst, ssem, rsem, dev).wait_recv()

    loads = []

    def load(src, dst):
        c = pltpu.make_async_copy(src, dst, load_sem.at[len(loads)])
        c.start()
        loads.append(c)
        return c

    small = [load(*p) for p in ((hid_h, hid), (len_h, len_s), (ids_h, ids), (gates_h, gates), (freq_h, freq), (ag_h, ag), (mg_h, mg))]
    proj = [load(wq_h, wq_v), load(wkv_h, wkv_v)]
    for r in range(n):
        pltpu.make_async_copy(kv_h.at[r], kv_v.at[r], kv_sem).start()
    load_o = load(wo_h, wo_v)
    own_gu = load(gu_h, raw.at[0])
    own_dn = load(dn_h, dn.at[0])

    barrier = pltpu.get_barrier_semaphore()
    peers = [(0, tc(k)) for k in range(1, n_tp)] + [(1, tc(k)) for k in range(n_tp)]
    far_rep = lambda side: rep if side == 0 else 1 - rep
    greet = [{"rep": far_rep(side), "tp": t} for side, t in peers]
    greet += [at(yc(k), z) for k in range(1, NY)] + [nbr[0], nbr[1], at(y, zc(opp))]
    for dev in greet:
        pl.semaphore_signal(barrier, inc=1, device_id=dev, device_id_type=MESH)
    pl.semaphore_wait(barrier, len(greet))

    for c in small:
        c.wait()
    for side, t in peers:
        send(hid, tok.at[side, tp], tok_send_sem.at[side], tok_recv_sem.at[side], {"rep": far_rep(side), "tp": t})
    tok[0, tp] = hid[...]
    send(gu_h, raw.at[1], wx_s.at[0], wx_r.at[0], partner)
    send(dn_h, dn.at[1], wx_s.at[1], wx_r.at[1], partner)

    slot = mig_s[0]
    row = lax.broadcasted_iota(jnp.int32, (n, 128), 0)
    lane = lax.broadcasted_iota(jnp.int32, (n, 128), 1)
    moved = row == slot
    own_span = rows_of(lambda r: jnp.where(rep == 0, len_s[0, r], len_s[1, r]), n)
    other_span = rows_of(lambda r: jnp.where(rep == 0, len_s[1, r], len_s[0, r]), n)
    span = jnp.where(moved, other_span, own_span).astype(f32)
    angle = span * freq[...]
    cosine, sine = jnp.cos(angle), jnp.sin(angle)
    first = lax.rem(lane, HEAD_SIZE) < HEAD_SIZE // 2
    half = HEAD_SIZE // 2

    def rotate(v):
        turned = jnp.where(first, -pltpu.roll(v, 128 - half, 1), pltpu.roll(v, half, 1))
        return v * cosine + turned * sine

    head = lax.broadcasted_iota(jnp.int32, bias_s.shape, 0)
    pos = lax.broadcasted_iota(jnp.int32, bias_s.shape, 1)
    bias_s[...] = jnp.where(lax.rem(pos, kvh) == head // group, 0.0, MASKED)

    eye = lax.broadcasted_iota(jnp.int32, (n, n), 0) == lax.broadcasted_iota(jnp.int32, (n, n), 1)
    expert = lax.rem(lane, GATE_LANES // 2)
    dense = jnp.zeros((n, 128), f32)
    for k in range(ids.shape[0]):
        idc = jnp.sum(jnp.where(eye, ids[k:k + 1, :], 0), axis=1, keepdims=True)
        gc = jnp.sum(jnp.where(eye, gates[k:k + 1, :], 0.0), axis=1, keepdims=True)
        dense = dense + jnp.where(expert == idc, gc, 0.0)
    high = dense.astype(bf).astype(f32)
    ga[z, y, :, 0:GATE_LANES] = jnp.where(lane < GATE_LANES // 2, high, dense - high).astype(bf)

    part = wide.shape[0]

    def split(j):
        def step(i, carry):
            start = pl.multiple_of(i * part, part)
            wide[...] = raw[j, pl.ds(start, part), :].astype(f32)
            rows = pl.ds(pl.multiple_of(i * (part // 2), part // 2), part // 2)
            gu[j, rows, 0:128] = wide[pl.ds(0, part // 2, stride=2), :].astype(bf)
            gu[j, rows, 128:256] = wide[pl.ds(1, part // 2, stride=2), :].astype(bf)
            return carry
        lax.fori_loop(0, raw.shape[1] // part, step, 0)

    took(tok.at[0, 0:n_tp - 1], tok_send_sem.at[0], tok_recv_sem.at[0], partner)
    took(tok.at[1], tok_send_sem.at[1], tok_recv_sem.at[1], partner)

    moved_w = lax.broadcasted_iota(jnp.int32, (n, width), 0) == slot
    tokens = jnp.concatenate(
        [jnp.where(moved_w, tok[1, t].astype(f32), tok[0, t].astype(f32)) for t in range(n_tp)], axis=1)
    mean = jnp.mean(tokens * tokens, axis=1, keepdims=True)
    gain = jnp.concatenate([ag[i:i + 1, :] for i in range(ag.shape[0])], axis=1)
    normed = (tokens * lax.rsqrt(mean + EPSILON) * gain).astype(bf)
    for c in proj:
        c.wait()
    queries = jnp.dot(normed, wq_v[...], preferred_element_type=f32)
    keyval = jnp.dot(normed, wkv_v[...], preferred_element_type=f32)
    q_s[...] = jnp.zeros_like(q_s)
    kvn_s[...] = jnp.zeros_like(kvn_s)
    low_lanes = lane < HEAD_SIZE
    for i in range(heads // 2):
        turned = rotate(queries[:, i * 128:(i + 1) * 128]).astype(bf).astype(f32)
        q_s[:, 2 * i, :] = jnp.where(low_lanes, turned, 0.0)
        q_s[:, 2 * i + 1, :] = jnp.where(low_lanes, pltpu.roll(turned, HEAD_SIZE, 1), 0.0)
    for g in range(kvh):
        both = keyval[:, g * 128:(g + 1) * 128]
        both = jnp.where(low_lanes, rotate(both), both).astype(bf).astype(f32)
        for h in range(g * group, (g + 1) * group):
            kvn_s[:, h, :] = both

    pltpu.make_async_copy(kv_h, kv_v, kv_sem).wait()
    kv_send[...] = kv_v[slot]
    kv_copy = rcopy(kv_send, kv_recv, kv_send_sem, kv_recv_sem, partner)
    kv_copy.start()

    def own_request(r):
        return q_s[r], kvn_s[r], kv_v[r], kvh * jnp.where(rep == 0, len_s[0, r], len_s[1, r])

    GROUP = 8

    def step(i, carry):
        rs = [i * GROUP + j for j in range(GROUP)]
        for r, o in zip(rs, attend([own_request(r) for r in rs], bias_s[...])):
            ctx_s[r] = o
        return carry

    lax.fori_loop(0, n // GROUP - 1, step, 0)
    kv_copy.wait()
    rs = list(range(n - GROUP, n))
    limit = kvh * jnp.where(rep == 0, len_s[1, slot], len_s[0, slot])
    last = attend([own_request(r) for r in rs] + [(q_s[slot], kvn_s[slot], kv_recv[...], limit)], bias_s[...])
    for r, o in zip(rs, last):
        ctx_s[r] = o
    arrived = last[-1]

    blocks = []
    for i in range(heads // 2):
        even = jnp.where(moved, arrived[2 * i:2 * i + 1], ctx_s[:, 2 * i, :])
        odd = jnp.where(moved, arrived[2 * i + 1:2 * i + 2], ctx_s[:, 2 * i + 1, :])
        blocks.append(jnp.where(low_lanes, pltpu.roll(even, HEAD_SIZE, 1), odd))
    context = jnp.concatenate(blocks, axis=1).astype(bf)
    load_o.wait()
    partial = jnp.dot(context, wo_v[...], preferred_element_type=f32)
    part_send[...] = partial.astype(bf)
    for k in (1, 3, 2):
        send(part_send, part_recv.at[tp], part_send_sem, part_recv_sem, {"tp": tc(k)})
    own_gu.wait()
    own_dn.wait()
    split(0)
    took(raw.at[1], wx_s.at[0], wx_r.at[0], partner)
    took(dn.at[1], wx_s.at[1], wx_r.at[1], partner)
    split(1)
    total = tokens + partial
    took(part_recv.at[0:n_tp - 1], part_send_sem, part_recv_sem, partner)
    for k in (1, 3, 2):
        total = total + part_recv[tc(k)].astype(f32)
    mean = jnp.mean(total * total, axis=1, keepdims=True)
    gain = jnp.concatenate([mg[i:i + 1, :] for i in range(mg.shape[0])], axis=1)
    x = (total * lax.rsqrt(mean + EPSILON) * gain).astype(bf)
    cut = a - GATE_LANES
    ga[z, y, :, GATE_LANES:] = x[:, 0:cut]
    gb[z, y] = x[:, cut:]

    ORDER = (0, 1, 3, 2)
    REL = ((0, 1), (3, 2))
    AWAY = (1, 3, 2)
    for d in (0, 1):
        send(gb.at[z, y], gb.at[z, y], b1_s.at[0], b1_r.at[d, 1], nbr[d])
    for k in AWAY:
        send(ga.at[z, y], ga.at[z, y], a1_s, a1_r.at[y], at(yc(k), z))
    for d in (0, 1):
        send(ga.at[z, y], ga.at[z, y], a2_s, a2_r.at[d, 1, 0], nbr[d])
    for k in AWAY:
        send(gb.at[z, y], gb.at[z, y], b2_s, b2_r.at[z], at(yc(k), z))
    own = jnp.zeros((n, width), f32)
    for t in range(n_tp):
        own = jnp.where(tp == t, total[:, t * width:(t + 1) * width], own)
    xf[n_tp] = own
    number = (rep * n_req + req, (1 - rep) * n_req + req)

    def compute(zs):
        rows_a = jnp.concatenate([ga[zz].reshape(NY * n, a) for zz in zs], axis=0)
        rows_b = jnp.concatenate([gb[zz].reshape(NY * n, b) for zz in zs], axis=0)
        table = rows_a[:, 0:GATE_LANES].astype(f32)
        which = lax.rem(lax.broadcasted_iota(jnp.int32, table.shape, 1), GATE_LANES // 2)
        acts = []
        for j in (0, 1):
            weight = jnp.sum(jnp.where(which == number[j], table, 0.0), axis=1, keepdims=True)
            pr = jnp.dot(rows_a[:, GATE_LANES:], gu[j, 0:cut, :], preferred_element_type=f32)
            pr = pr + jnp.dot(rows_b, gu[j, cut:cut + b, :], preferred_element_type=f32)
            g, u = pr[:, 0:128], pr[:, 128:256]
            acts.append((g / (1.0 + jnp.exp(-g)) * u * weight).astype(bf))
        o = jnp.dot(acts[0], dn[0], preferred_element_type=f32) + jnp.dot(acts[1], dn[1], preferred_element_type=f32)
        for i, zz in enumerate(zs):
            block = o[i * NY * n:(i + 1) * NY * n]
            pa[zz] = block[:, 0:fa].reshape(NY, n, fa)
            pb[zz] = block[:, fa:].reshape(NY, n, fb)
            by_s[zz] = block[:, fa:].astype(bf).reshape(NY, n, fb)
            for k in AWAY:
                send(by_s.at[zz, yc(k)], by_r.at[zz, y], rby_s, rby_r.at[zz], at(yc(k), z))

    def chunks(*steps):
        zs = []
        for s in steps:
            zs += [zc(s)] if s in (0, opp) else [zc(-s), zc(s)]
        for zz in zs:
            took(gb.at[zz, 0:NY - 1], b2_s, b2_r.at[zz], partner)
        compute(zs)

    def a_send(d, k, i, value):
        sa[d * (opp + 1) + k, i] = value.astype(bf)
        send(sa.at[d * (opp + 1) + k, i], ra.at[d, k, i], rsa_s, rsa_r.at[d, k, i], nbr[d])

    def a_took(d, k, i):
        took(ra.at[d, k, i], rsa_s, rsa_r.at[d, k, i], nbr[d])
        return ra[d, k, i].astype(f32)

    def pass_b(s):
        for d in (0, 1):
            zz = zc(-s) if d == 0 else zc(s)
            if s < opp:
                took(gb.at[zz, y], b1_s.at[0], b1_r.at[d, s], nbr[d])
                block = gb.at[zz, y] if s + 1 < opp else gb.at[zz, y, :, part_b[d]]
                send(block, block, b1_s.at[0 if s + 1 < opp else 1], b1_r.at[d, s + 1], nbr[d])
            else:
                took(gb.at[zz, y, :, part_b[d]], b1_s.at[0], b1_r.at[d, s], nbr[d])
        for d in (0, 1) if s < opp else (0,):
            zz = zc(-s) if d == 0 else zc(s)
            for k in AWAY:
                send(gb.at[zz, y], gb.at[zz, y], b2_s, b2_r.at[zz], at(yc(k), z))

    def pass_a(s):
        for i in ORDER:
            for d in (0, 1):
                if s == opp and i not in REL[d]:
                    continue
                zz = zc(-s) if d == 0 else zc(s)
                yb = yc(i)
                if s:
                    took(ga.at[zz, yb], a2_s, a2_r.at[d, s, i], nbr[d])
                elif i == 0:
                    continue
                elif d == 0:
                    took(ga.at[z, yb], a1_s, a1_r.at[yb], at(yb, z))
                if s + 1 < opp or (s + 1 == opp and i in REL[d]):
                    send(ga.at[zz, yb], ga.at[zz, yb], a2_s, a2_r.at[d, s + 1, i], nbr[d])

    pass_b(1)
    pass_a(0)
    pass_b(2)
    pass_a(1)
    pass_b(3)
    pass_a(2)
    pass_b(4)
    chunks(0, 1)
    pass_a(3)
    chunks(2, 3)
    for d in (0, 1):
        for i in REL[1 - d]:
            a_send(d, opp - 1, i, pa[zc(opp - 1) if d == 0 else zc(1 - opp), yc(i)])
    pass_a(4)
    chunks(4)

    def a_step(k):
        for i in ORDER:
            for d in (0, 1):
                if k >= opp - 1 and i not in REL[d]:
                    continue
                value = pa[zc(k) if d == 0 else zc(-k), yc(i)]
                if k < opp:
                    value = value + a_took(d, k + 1, i)
                a_send(d, k, i, value)

    def b_own(zz):
        value = pb[zz, y]
        took(by_r.at[zz, 0:NY - 1], rby_s, rby_r.at[zz], partner)
        for k in AWAY:
            value = value + by_r[zz, yc(k)].astype(f32)
        return value

    def b_step(k):
        if k == opp:
            sb[0, k] = b_own(zc(k)).astype(bf)
            send(sb.at[0, k], rb.at[0, k], rsb_s.at[1], rsb_r.at[0, k], at(y, zc(k)))
            return
        for d in (0, 1):
            value = b_own(zc(k) if d == 0 else zc(-k))
            if k < opp - 1:
                took(rb.at[d, k + 1], rsb_s.at[0], rsb_r.at[d, k + 1], nbr[d])
                value = value + rb[d, k + 1].astype(f32)
            sb[d, k] = value.astype(bf)
            send(sb.at[d, k], rb.at[d, k], rsb_s.at[0], rsb_r.at[d, k], nbr[d])

    a_step(4)
    b_step(3)
    a_step(3)
    b_step(2)
    b_step(4)
    a_step(2)
    b_step(1)
    a_step(1)
    for k in AWAY:
        yb = yc(k)
        ys[yb] = (pa[z, yb] + a_took(0, 1, k) + a_took(1, 1, k)).astype(bf)
        send(ys.at[yb], yr.at[y], ry_s, ry_r, at(yb, z))
    total_a = pa[z, y] + a_took(0, 1, 0) + a_took(1, 1, 0)
    total_b = b_own(z)
    for d in (0, 1):
        took(rb.at[d, 1], rsb_s.at[0], rsb_r.at[d, 1], nbr[d])
        total_b = total_b + rb[d, 1].astype(f32)
    took(rb.at[0, opp], rsb_s.at[1], rsb_r.at[0, opp], at(y, zc(opp)))
    total_b = total_b + rb[0, opp].astype(f32)
    took(yr.at[0:NY - 1], ry_s, ry_r, partner)
    for k in AWAY:
        total_a = total_a + yr[yc(k)].astype(f32)

    total = jnp.concatenate([total_a, total_b], axis=1)
    for t in range(n_tp):
        quarter = total[:, t * width:(t + 1) * width]
        xf[t] = quarter
        xs[t] = quarter.astype(bf)
    for k in AWAY:
        t = tc(k)
        send(xs.at[t], xr.at[tp], rx_s, rx_r, {"tp": t})
    value = xf[n_tp] + xf[tp]
    took(xr.at[0:n_tp - 1], rx_s, rx_r, partner)
    for k in AWAY:
        value = value + xr[tc(k)].astype(f32)
    out[...] = value.astype(bf)
    sent(tok.at[0, 0:n_tp - 1], tok_send_sem.at[0])
    sent(tok.at[1], tok_send_sem.at[1])
    sent(raw.at[0], wx_s.at[0])
    sent(dn.at[0], wx_s.at[1])
    sent(part_recv.at[0:n_tp - 1], part_send_sem)
    sent(ga.at[0, 0:NY - 1], a1_s)
    sent(ga.at[0:NZ - 1], a2_s)
    sent(gb.at[0:opp - 1, 0:2], b1_s.at[0])
    sent(gb.at[0, 0], b1_s.at[1])
    sent(gb.at[0:NZ - 2], b2_s)
    sent(by_s.at[0:NZ - 2], rby_s)
    sent(sa.at[0:NZ - 1], rsa_s)
    sent(sb.at[:, 0:opp - 1], rsb_s.at[0])
    sent(sb.at[0, 0], rsb_s.at[1])
    sent(ys.at[0:NY - 1], ry_s)
    sent(xs.at[0:n_tp - 1], rx_s)


def layer(
    hidden, lengths, migrate, kv_cache, attn_gain, moe_gain, w_query, key_value_weight, output_weight,
    w_gateup, w_down, expert_ids, expert_gates,
):
    n_tp, n_req = lax.axis_size("tp"), lax.axis_size("req")
    n, width = hidden.shape
    model = w_query.shape[0]
    kvh = kv_cache.shape[2]
    kv = kv_cache.reshape(n, kv_cache.shape[1] * kvh, kv_cache.shape[3])
    lanes = kv.shape[1]
    i = np.arange(128) % (HEAD_SIZE // 2)
    freq = jnp.asarray((ROPE_BASE ** (-2.0 * i / HEAD_SIZE)).astype(np.float32)[None])
    ag, mg = attn_gain.reshape(-1, 128), moe_gain.reshape(-1, 128)
    ids, gates = expert_ids.T, expert_gates.T
    a, fa = A_LANES, FA_LANES
    b, fb = GATE_LANES + model - a, model - fa
    gu = w_gateup.reshape(2 * model, w_gateup.shape[3])
    dn = w_down[0]
    bf, f32 = jnp.bfloat16, jnp.float32
    dma, v = pltpu.SemaphoreType.DMA, pltpu.VMEM
    k5 = NZ // 2 + 1
    args = (lengths, migrate, hidden, kv, ag, mg, freq, w_query, key_value_weight, output_weight, ids, gates, gu, dn)
    return pl.pallas_call(
        functools.partial(layer_kernel, n_tp, n_req),
        name="layer",
        out_shape=jax.ShapeDtypeStruct((n, width), bf),
        in_specs=[pl.BlockSpec(memory_space=pltpu.SMEM if i == 1 else pltpu.HBM) for i in range(len(args))],
        out_specs=pl.BlockSpec(memory_space=pltpu.VMEM),
        scratch_shapes=[
            pltpu.SMEM(lengths.shape, jnp.int32),
            v(hidden.shape, bf), v(ag.shape, f32), v(mg.shape, f32), v(freq.shape, f32), v(ids.shape, jnp.int32), v(gates.shape, f32),
            v(kv.shape, bf), v(w_query.shape, bf), v(key_value_weight.shape, bf), v(output_weight.shape, bf),
            v((2, n_tp, n, width), bf), v(kv.shape[1:], bf), v(kv.shape[1:], bf), v((n, model), bf), v((n_tp, n, model), bf),
            v((n, 8, 128), f32), v((n, 8, 128), f32), v((n, 8, 128), f32), v((8, lanes), f32),
            v((NZ, NY, n, a), bf), v((NZ, NY, n, b), bf), v((NZ, NY, n, fa), f32), v((NZ, NY, n, fb), f32),
            v((2,) + gu.shape, bf), v((512, 128), f32), v((2, model, 256), bf), v((2,) + dn.shape, bf),
            v((NZ, NY, n, fb), bf), v((NZ, NY, n, fb), bf),
            v((2 * k5, NY, n, fa), bf), v((2, k5, NY, n, fa), bf), v((2, k5, n, fb), bf), v((2, k5, n, fb), bf),
            v((NY, n, fa), bf), v((NY, n, fa), bf), v((n_tp, n, width), bf), v((n_tp, n, width), bf), v((n_tp + 1, n, width), f32),
            dma((12,)), dma, dma((2,)), dma((2,)), dma, dma, dma, dma,
            dma((2,)), dma((2,)), dma, dma((NY,)), dma, dma((2, k5, NY)), dma((2,)), dma((2, k5)), dma, dma((NZ,)),
            dma, dma((NZ,)), dma, dma((2, k5, NY)), dma((2,)), dma((2, k5)), dma, dma, dma, dma,
        ],
        compiler_params=pltpu.CompilerParams(collective_id=0, has_side_effects=True, vmem_limit_bytes=VMEM_LIMIT),
        cost_estimate=pl.CostEstimate(flops=1_500_000_000, bytes_accessed=16_000_000, transcendentals=1_000_000),
    )(*args)


def solution(mesh):
    placed = (
        P(("rep", "req"), "tp"),
        P(None, "req"),
        P("req"),
        P(("rep", "req"), None, "tp", None),
        P(),
        P(),
        P(None, "tp"),
        P(None, "tp"),
        P("tp", None),
        P(("rep", "req"), None, None, "tp"),
        P(("rep", "req"), "tp", None),
        P(("rep", "req"), None),
        P(("rep", "req"), None),
    )
    return jax.shard_map(
        layer, mesh=mesh, in_specs=placed, out_specs=P(("rep", "req"), "tp"), check_vma=False
    )
```
